32 devices in a mesh: dp: 8 (over z, x), seq: 4 (over y, core).
Axes of the slice: x: 2, y: 2, z: 4, core: 2. Of those that a mesh axis runs over, the one named last changes fastest.
Arguments:
- inputs: bfloat16 [16, 512, 1536], P('dp', 'seq'), may hold values from -6 to 6
- conditioning: bfloat16 [16, 128, 1536], P('dp', 'seq'), may hold values from -6 to 6
- seq_lengths: int32 [16], P('dp'), may hold values from 128 to 512, as said below
- cond_lengths: int32 [16], P('dp'), may hold values from 32 to 128, as said below
- gain_self: bfloat16 [1536], P(('dp', 'seq')), may hold values from 0.5 to 1.5
- gain_cross: bfloat16 [1536], P(('dp', 'seq')), may hold values from 0.5 to 1.5
- gain_mlp: bfloat16 [1536], P(('dp', 'seq')), may hold values from 0.5 to 1.5
- w_query: bfloat16 [1536, 1536], P(('dp', 'seq')), may hold values from -0.15625 to 0.15625
- w_key: bfloat16 [1536, 1536], P(('dp', 'seq')), may hold values from -0.15625 to 0.15625
- w_value: bfloat16 [1536, 1536], P(('dp', 'seq')), may hold values from -0.15625 to 0.15625
- w_output: bfloat16 [1536, 1536], P(('dp', 'seq')), may hold values from -2 to 2
- c_query: bfloat16 [1536, 1536], P(('dp', 'seq')), may hold values from -0.15625 to 0.15625
- c_key: bfloat16 [1536, 1536], P(('dp', 'seq')), may hold values from -0.15625 to 0.15625
- c_value: bfloat16 [1536, 1536], P(('dp', 'seq')), may hold values from -0.15625 to 0.15625
- c_output: bfloat16 [1536, 1536], P(('dp', 'seq')), may hold values from -1 to 1
- w_gate: bfloat16 [1536, 6144], P(('dp', 'seq')), may hold values from -0.15625 to 0.15625
- w_up: bfloat16 [1536, 6144], P(('dp', 'seq')), may hold values from -0.15625 to 0.15625
- w_down: bfloat16 [1536, 6144], P(('dp', 'seq')), may hold values from -0.078125 to 0.078125
- cotangent: bfloat16 [16, 512, 1536], P('dp', 'seq'), may hold values from -6 to 6
Outputs:
- block_out: bfloat16 [16, 512, 1536], P('dp', 'seq')
- grad_inputs: float32 [16, 512, 1536], P('dp', 'seq')
- grad_conditioning: float32 [16, 128, 1536], P('dp', 'seq')
- grad_gain_self: float32 [1536], P(('dp', 'seq'))
- grad_gain_cross: float32 [1536], P(('dp', 'seq'))
- grad_gain_mlp: float32 [1536], P(('dp', 'seq'))
- grad_w_query: float32 [1536, 1536], P(('dp', 'seq'))
- grad_w_key: float32 [1536, 1536], P(('dp', 'seq'))
- grad_w_value: float32 [1536, 1536], P(('dp', 'seq'))
- grad_w_output: float32 [1536, 1536], P(('dp', 'seq'))
- grad_c_query: float32 [1536, 1536], P(('dp', 'seq'))
- grad_c_key: float32 [1536, 1536], P(('dp', 'seq'))
- grad_c_value: float32 [1536, 1536], P(('dp', 'seq'))
- grad_c_output: float32 [1536, 1536], P(('dp', 'seq'))
- grad_w_gate: float32 [1536, 6144], P(('dp', 'seq'))
- grad_w_up: float32 [1536, 6144], P(('dp', 'seq'))
- grad_w_down: float32 [1536, 6144], P(('dp', 'seq'))
The draws below stay inside these ranges and needn't reach their ends.
Inputs may be any that keep to these rules, and one draw needn't show every extreme that they name: The valid tokens of a sequence are its first seq_lengths slots; some sequence has all 512. The valid conditioning tokens are the first cond_lengths slots; some sequence has all 128.
All inputs are finite; a program needn't handle non-finite values.
Results may differ from the reference program's by a relative error of at most 0.025.
Values may be sent and summed in bfloat16 or wider, within the bound.
A program may use at most 320 MiB of HBM per device.

```python
import jax
import jax.numpy as jnp
from jax import lax

D = 1536
HEADS = 24
HEAD = 64
FF = 6144
ROT = 32
LEN = 512
CONDS = 128
SEQS = 16


def draw_seq_lengths(key, part):
    key_one = jax.random.fold_in(key, 11)
    key_two = jax.random.fold_in(key, 12)
    drawn = jax.random.randint(key_one, (SEQS,), LEN // 4, LEN + 1)
    chosen = jax.random.randint(key_two, (), 0, SEQS)
    return jnp.where(jnp.arange(SEQS) == chosen, LEN, drawn).astype(jnp.int32)


def draw_cond_lengths(key, part):
    key_one = jax.random.fold_in(key, 21)
    key_two = jax.random.fold_in(key, 22)
    drawn = jax.random.randint(key_one, (SEQS,), CONDS // 4, CONDS + 1)
    chosen = jax.random.randint(key_two, (), 0, SEQS)
    return jnp.where(jnp.arange(SEQS) == chosen, CONDS, drawn).astype(jnp.int32)


def block_levels(rng, extent, cuts, smallest, top_value):
    loudness = 1.0
    for position, blocks in cuts:
        steps = jax.random.uniform(jax.random.fold_in(jax.random.fold_in(rng, 6), position), (blocks,), jnp.float32, smallest / len(cuts), top_value / len(cuts))
        loudness = loudness * jnp.repeat(jnp.exp(steps), extent[position] // blocks).reshape((-1,) + (1,) * (len(extent) - 1 - position))
    return loudness


def gaussian(rng, dims, deviation, bound, cuts=(), kind=jnp.bfloat16):
    gain = block_levels(rng, dims, cuts, -0.22, 0.18) if cuts else 1.0
    values = jax.random.normal(rng, dims, jnp.float32) * deviation * gain
    return jnp.minimum(jnp.maximum(values, -bound), bound).astype(kind)


def setup_inputs(seed: int = 0) -> dict:
    seeds = jax.random.split(jax.random.key(seed), 20)
    inputs = gaussian(seeds[0], (SEQS, LEN, D), 1.0, 6.0, ((0, 8), (1, 4)))
    conditioning = gaussian(seeds[1], (SEQS, CONDS, D), 1.0, 6.0, ((0, 8), (1, 4)))
    seq_lengths = draw_seq_lengths(jax.random.fold_in(seeds[19], 71), 0)
    cond_lengths = draw_cond_lengths(jax.random.fold_in(seeds[19], 71), 0)
    gain_self = jnp.clip(1.0 + 0.1 * jax.random.normal(seeds[4], (D,), jnp.float32), 0.5, 1.5).astype(jnp.bfloat16)
    gain_cross = jnp.clip(1.0 + 0.1 * jax.random.normal(seeds[5], (D,), jnp.float32), 0.5, 1.5).astype(jnp.bfloat16)
    gain_mlp = jnp.clip(1.0 + 0.1 * jax.random.normal(seeds[6], (D,), jnp.float32), 0.5, 1.5).astype(jnp.bfloat16)
    w_query = gaussian(seeds[7], (D, D), D ** -0.5, 0.15625, ((0, 32),))
    w_key = gaussian(seeds[8], (D, D), D ** -0.5, 0.15625, ((0, 32),))
    w_value = gaussian(seeds[9], (D, D), D ** -0.5, 0.15625, ((0, 32),))
    w_output = gaussian(seeds[10], (D, D), (max(D // 192, 2)) ** -0.5, 2.0, ((0, 32),))
    c_query = gaussian(seeds[11], (D, D), D ** -0.5, 0.15625, ((0, 32),))
    c_key = gaussian(seeds[12], (D, D), D ** -0.5, 0.15625, ((0, 32),))
    c_value = gaussian(seeds[13], (D, D), D ** -0.5, 0.15625, ((0, 32),))
    c_output = gaussian(seeds[14], (D, D), (max(D // 48, 2)) ** -0.5, 1.0, ((0, 32),))
    w_gate = gaussian(seeds[15], (D, FF), D ** -0.5, 0.15625, ((0, 32),))
    w_up = gaussian(seeds[16], (D, FF), D ** -0.5, 0.15625, ((0, 32),))
    w_down = gaussian(seeds[17], (D, FF), FF ** -0.5, 0.078125, ((0, 32),))
    cotangent = gaussian(seeds[18], (SEQS, LEN, D), 1.0, 6.0, ((0, 8), (1, 4)))
    return {"inputs": inputs, "conditioning": conditioning, "seq_lengths": seq_lengths, "cond_lengths": cond_lengths, "gain_self": gain_self, "gain_cross": gain_cross, "gain_mlp": gain_mlp, "w_query": w_query, "w_key": w_key, "w_value": w_value, "w_output": w_output, "c_query": c_query, "c_key": c_key, "c_value": c_value, "c_output": c_output, "w_gate": w_gate, "w_up": w_up, "w_down": w_down, "cotangent": cotangent}


@jax.custom_vjp
def low(v):
    return lax.optimization_barrier(v.astype(jnp.bfloat16)).astype(jnp.float32)

@jax.custom_vjp
def low_back(v):
    return v

def low_keep(v):
    return (low(v), None)

def low_pass(kept, grad):
    return (grad,)

def back_keep(v):
    return (v, None)

def back_low(kept, grad):
    return (low(grad),)
low.defvjp(low_keep, low_pass)
low_back.defvjp(back_keep, back_low)
HIGH = lax.Precision.HIGHEST

def matmul(left, right):
    return jnp.dot(left, right, precision=HIGH)

def layer_norm(values, gain_vec):
    average = lax.optimization_barrier(jnp.mean(values, axis=-1, keepdims=True))
    centred = values - average
    variance = lax.optimization_barrier(jnp.mean(centred * centred, axis=-1, keepdims=True))
    return centred * lax.rsqrt(variance + 1e-05) * gain_vec

def rotate(shaped, cosine, sine_table):
    half_rot = ROT // 2
    lower_half = shaped[..., :half_rot]
    upper_half = shaped[..., half_rot:ROT]
    return jnp.concatenate([lower_half * cosine - upper_half * sine_table, upper_half * cosine + lower_half * sine_table, shaped[..., ROT:]], axis=-1)

def attention(queries, key_rows, values, key_ok):
    scores = jnp.einsum('thd,shd->hts', queries, key_rows, precision=HIGH) * (1.0 / HEAD ** 0.5)
    scores = jnp.where(key_ok[None, None, :], scores, -1e+30)
    scores = low_back(scores)
    weights_soft = low(jax.nn.softmax(scores, axis=-1))
    return jnp.einsum('hts,shd->thd', weights_soft, values, precision=HIGH)

def block(tokens, condition, params, key_ok, cond_ok, cosine, sine_table):
    gain_one, gain_two, gain_three, query_w, key_w, value_w, output_w, cquery_w, ckey_w, cvalue_w, coutput_w, gate_w, up_w, down_w = params
    normed = low(layer_norm(tokens, gain_one))
    queries = low(rotate(low_back(matmul(normed, query_w)).reshape(LEN, HEADS, HEAD), cosine, sine_table))
    key_rows = low(rotate(low_back(matmul(normed, key_w)).reshape(LEN, HEADS, HEAD), cosine, sine_table))
    values = low(low_back(matmul(normed, value_w))).reshape(LEN, HEADS, HEAD)
    attended = low(low_back(attention(queries, key_rows, values, key_ok).reshape(LEN, D)))
    after_self = tokens + low_back(matmul(attended, output_w))
    normed_two = low(layer_norm(after_self, gain_two))
    cross_q = low(low_back(matmul(normed_two, cquery_w))).reshape(LEN, HEADS, HEAD)
    cross_k = low(low_back(matmul(condition, ckey_w))).reshape(CONDS, HEADS, HEAD)
    cross_v = low(low_back(matmul(condition, cvalue_w))).reshape(CONDS, HEADS, HEAD)
    cross_att = low(low_back(attention(cross_q, cross_k, cross_v, cond_ok).reshape(LEN, D)))
    after_cross = after_self + low_back(matmul(cross_att, coutput_w))
    normed_three = low(layer_norm(after_cross, gain_three))
    gate = low_back(matmul(normed_three, gate_w))
    up_vals = low_back(matmul(normed_three, up_w))
    hidden = low(jax.nn.silu(gate) * up_vals)
    branch = lax.dot_general(hidden, down_w, (((1,), (1,)), ((), ())), precision=HIGH)
    return after_cross + low_back(branch)

def reference(inputs, conditioning, seq_lengths, cond_lengths, gain_self, gain_cross, gain_mlp, w_query, w_key, w_value, w_output, c_query, c_key, c_value, c_output, w_gate, w_up, w_down, cotangent):
    params = tuple((item.astype(jnp.float32) for item in (gain_self, gain_cross, gain_mlp, w_query, w_key, w_value, w_output, c_query, c_key, c_value, c_output, w_gate, w_up, w_down)))
    half_rot = ROT // 2
    positions = jnp.arange(LEN).astype(jnp.float32)
    inverse = 10000.0 ** (-jnp.arange(half_rot).astype(jnp.float32) / half_rot)
    angles = positions[:, None] * inverse[None, :]
    cosine = jnp.cos(angles)[:, None, :]
    sine_table = jnp.sin(angles)[:, None, :]

    def one_sequence(totals, items):
        tokens, condition, length, cond_len, incoming = items
        key_ok = jnp.arange(LEN).astype(jnp.int32) < length
        cond_ok = jnp.arange(CONDS).astype(jnp.int32) < cond_len

        def apply(tok_rows, cond_rows, prm):
            return block(tok_rows, cond_rows, prm, key_ok, cond_ok, cosine, sine_table)
        result, pullback = jax.vjp(apply, tokens.astype(jnp.float32), condition.astype(jnp.float32), params)
        grad_tok, grad_cond, grad_params = pullback(incoming.astype(jnp.float32))
        totals = jax.tree.map(lambda total, extra: total + extra, totals, grad_params)
        return (totals, (result.astype(jnp.bfloat16), grad_tok, grad_cond))
    zeros = jax.tree.map(jnp.zeros_like, params)
    totals, stacked = lax.scan(one_sequence, zeros, (inputs, conditioning, seq_lengths, cond_lengths, cotangent))
    return (stacked[0], stacked[1], stacked[2], totals[0], totals[1], totals[2], totals[3], totals[4], totals[5], totals[6], totals[7], totals[8], totals[9], totals[10], totals[11], totals[12], totals[13])
```

```python
import functools
import math

import jax
import jax.numpy as jnp
from jax import lax
from jax.experimental import pallas as pl
from jax.experimental.pallas import tpu as pltpu
from jax.sharding import PartitionSpec as P

HEADS = 24
HEAD = 64
ROT = 32
EPSILON = 1e-05
BF = jnp.bfloat16
F32 = jnp.float32
PAIR = 2 * HEAD


def mm(left, right):
    return jnp.dot(left, right, preferred_element_type=F32)


def mm_t(left, right):
    return lax.dot_general(left, right, (((1,), (1,)), ((), ())), preferred_element_type=F32)


def t_mm(left, right):
    return lax.dot_general(left, right, (((0,), (0,)), ((), ())), preferred_element_type=F32)


def seq_swap(x, mask):
    n = lax.axis_size("seq")
    return lax.ppermute(x, "seq", [(i, i ^ mask) for i in range(n)])


def dp_swap(x, mask):
    n = lax.axis_size("dp")
    return lax.ppermute(x, "dp", [(i, i ^ mask) for i in range(n)])


def all_sum(v):
    for mask in (1, 2):
        v = v + seq_swap(v, mask)
    mask = 1
    while mask < lax.axis_size("dp"):
        v = v + dp_swap(v, mask)
        mask *= 2
    return v


def gather_seq(x):
    core = seq_swap(x, 1)
    far = seq_swap(x, 2)
    diag = seq_swap(far, 1)
    return jnp.stack([x, core, far, diag])


def scatter_seq(partial):
    far = partial[2].astype(F32) + seq_swap(partial[3], 1).astype(F32)
    arrived = seq_swap(far.astype(BF), 2)
    near = partial[0].astype(F32) + seq_swap(partial[1], 1).astype(F32)
    return near + arrived.astype(F32)


RING_Z, RING_X = 4, 2


def ringed():
    return lax.axis_size("dp") == RING_Z * RING_X


def z_next(x):
    n = lax.axis_size("dp")
    return lax.ppermute(x, "dp", [(i, (i + RING_X) % n) for i in range(n)])


def ring_pieces(x):
    d = lax.axis_index("dp")
    z, xx = d // RING_X, d % RING_X
    held = x
    for k in range(RING_Z):
        zk = (z + RING_Z - k) % RING_Z
        yield zk * RING_X + xx, held
        yield zk * RING_X + 1 - xx, dp_swap(held, 1)
        if k < RING_Z - 1:
            held = z_next(held)


def gather_dp(chunk):
    if not ringed():
        return lax.all_gather(chunk, "dp", axis=0, tiled=True)
    rows, cols = chunk.shape
    out = jnp.zeros((rows * lax.axis_size("dp"), cols), chunk.dtype)
    for index, piece in ring_pieces(chunk):
        out = lax.dynamic_update_slice(out, piece, (index * rows, 0))
    return out


def reduce_dp(slots):
    if not ringed():
        n, rows, cols = slots.shape
        return lax.psum_scatter(
            slots.reshape(n * rows, cols), "dp", scatter_dimension=0, tiled=True
        ).astype(F32)
    d = lax.axis_index("dp")
    z, xx = d // RING_X, d % RING_X
    n, rows, cols = slots.shape
    split = slots.reshape(RING_Z, RING_X, rows, cols)
    away = lax.dynamic_index_in_dim(split, 1 - xx, axis=1, keepdims=False)
    kept = lax.dynamic_index_in_dim(split, xx, axis=1, keepdims=False)
    arrived = dp_swap(away, 1)
    both = (kept.astype(F32) + arrived.astype(F32)).astype(BF)

    def at(k):
        return lax.dynamic_index_in_dim(both, (z + RING_Z - k) % RING_Z, axis=0, keepdims=False)

    total = at(1)
    for k in range(2, RING_Z + 1):
        total = z_next(total.astype(BF)).astype(F32) + at(k).astype(F32)
    return total


def columns_out(x):
    rows = x.shape[0]
    n = lax.axis_size("seq")
    return x.reshape(rows, HEADS // n, n, HEAD).transpose(2, 0, 1, 3).reshape(n, rows, -1)


def columns_back(x):
    n, rows, _ = x.shape
    return x.reshape(n, rows, HEADS // n, HEAD).transpose(1, 2, 0, 3).reshape(rows, HEADS * HEAD)


def blocks_out(x):
    rows = x.shape[0]
    n = lax.axis_size("seq")
    return x.reshape(rows, n, -1).transpose(1, 0, 2)


def blocks_back(x):
    return x.transpose(1, 0, 2).reshape(x.shape[1], -1)


def deal(x):
    got = lax.all_to_all(x, "seq", split_axis=0, concat_axis=0, tiled=True)
    return got.reshape(-1, x.shape[-1])


def collect(x):
    n = lax.axis_size("seq")
    return lax.all_to_all(
        x.reshape(n, -1, x.shape[-1]), "seq", split_axis=0, concat_axis=0, tiled=True
    )


def head_slot():
    s, d = lax.axis_index("seq"), lax.axis_index("dp")
    n = lax.axis_size("seq")
    per = HEADS // lax.axis_size("dp")
    return (s + (n - per % n) * d) % n, per, n


def slot_place(d):
    s = lax.axis_index("seq")
    n = lax.axis_size("seq")
    per = HEADS // lax.axis_size("dp")
    j = (s + (n - per % n) * d) % n
    return jnp.where(j < per, (per * d + j - s) // n, HEADS // n)


def gather_head_rows(x):
    n = lax.axis_size("seq")
    s = lax.axis_index("seq")
    cols = x.shape[1]
    mine = HEADS // n
    if not ringed():
        full = lax.all_gather(x, ("dp", "seq"), axis=0, tiled=True)
        picked = lax.dynamic_index_in_dim(full.reshape(mine, n, HEAD, cols), s, 1, keepdims=False)
        return picked.reshape(mine * HEAD, cols)
    rows = lax.all_gather(x, "seq", axis=0, tiled=True)
    j, per, _ = head_slot()
    rows = jnp.concatenate([rows, jnp.zeros((HEAD, cols), x.dtype)])
    piece = lax.dynamic_slice(rows, (j * HEAD, 0), (HEAD, cols))
    out = jnp.zeros(((mine + 1) * HEAD, cols), x.dtype)
    for index, held in ring_pieces(piece):
        out = lax.dynamic_update_slice(out, held, (slot_place(index) * HEAD, 0))
    return out[: mine * HEAD]


def reduce_head_rows(x):
    n = lax.axis_size("seq")
    s = lax.axis_index("seq")
    size = lax.axis_size("dp")
    cols = x.shape[1]
    mine = HEADS // n
    if not ringed():
        full = jnp.zeros((mine, n, HEAD, cols), BF)
        full = lax.dynamic_update_index_in_dim(full, x.reshape(mine, 1, HEAD, cols), s, 1)
        return lax.psum_scatter(
            full.reshape(-1, cols), ("dp", "seq"), scatter_dimension=0, tiled=True
        ).astype(F32)
    padded = jnp.concatenate([x, jnp.zeros((HEAD, cols), x.dtype)])
    slots = jnp.stack(
        [lax.dynamic_slice(padded, (slot_place(d) * HEAD, 0), (HEAD, cols)) for d in range(size)]
    )
    own = reduce_dp(slots).astype(BF)
    pieces = lax.all_gather(own, "seq", axis=0, tiled=False)
    per = HEADS // size
    d = lax.axis_index("dp")
    rows = jnp.concatenate(
        [
            lax.dynamic_index_in_dim(pieces, (per * d + j) % n, 0, keepdims=False)
            for j in range(per)
        ]
    )
    share = per * HEAD // n
    return lax.dynamic_slice(rows, (s * share, 0), (share, cols)).astype(F32)


def norm_forward(values, gain_vec):
    average = jnp.mean(values, axis=-1, keepdims=True)
    centred = values - average
    variance = jnp.mean(centred * centred, axis=-1, keepdims=True)
    inv_std = lax.rsqrt(variance + EPSILON)
    normal = centred * inv_std
    return normal, inv_std, (normal * gain_vec).astype(BF)


def norm_backward(grad_normed, normal, inv_std, gain_vec):
    grad_gain = jnp.sum(grad_normed * normal, axis=0)
    grad_hat = grad_normed * gain_vec
    mean_hat = jnp.mean(grad_hat, axis=-1, keepdims=True)
    mean_mix = jnp.mean(grad_hat * normal, axis=-1, keepdims=True)
    return inv_std * (grad_hat - mean_hat - normal * mean_mix), grad_gain


def flat(ref):
    value = ref[...]
    return value.reshape(value.shape[0] * value.shape[1] * value.shape[2], value.shape[3])


def turn(m, cos, up, down):
    return m * cos + pltpu.roll(m, PAIR - ROT // 2, 1) * up + pltpu.roll(m, ROT // 2, 1) * down


SCALE = 1.0 / math.sqrt(HEAD)


def soft(q, k, ok):
    scores = mm_t(q, k) * SCALE
    scores = jnp.where(ok > 0.0, scores, -1e30)
    top = jnp.max(scores, axis=-1, keepdims=True)
    e = jnp.exp(scores - top)
    return e * (1.0 / jnp.sum(e, axis=-1, keepdims=True))


def self_forward_kernel(ok_ref, cos_ref, up_ref, down_ref, q_ref, k_ref, v_ref, o_ref, qr_ref, kr_ref, vr_ref):
    cos, up, down = (r[...].reshape(-1, PAIR) for r in (cos_ref, up_ref, down_ref))
    q = turn(flat(q_ref), cos, up, down).astype(BF)
    k = turn(flat(k_ref), cos, up, down).astype(BF)
    v = flat(v_ref).astype(BF)
    ok = ok_ref[0]
    outs = []
    for h in (0, 1):
        sl = slice(h * HEAD, (h + 1) * HEAD)
        p = soft(q[:, sl], k[:, sl], ok).astype(BF)
        outs.append(mm(p, v[:, sl]))
    o_ref[...] = jnp.concatenate(outs, axis=1).astype(BF).reshape(o_ref.shape)
    qr_ref[...] = q.reshape(qr_ref.shape)
    kr_ref[...] = k.reshape(kr_ref.shape)
    vr_ref[...] = v.reshape(vr_ref.shape)


def pair_back(q, k, v, g, ok):
    dqs, dks, dvs = [], [], []
    for h in (0, 1):
        sl = slice(h * HEAD, (h + 1) * HEAD)
        p = soft(q[:, sl], k[:, sl], ok)
        dp = mm_t(g[:, sl], v[:, sl])
        inner = jnp.sum(p * dp, axis=-1, keepdims=True)
        ds = (p * (dp - inner)).astype(BF)
        dqs.append(mm(ds, k[:, sl]) * SCALE)
        dks.append(t_mm(ds, q[:, sl]) * SCALE)
        dvs.append(t_mm(p.astype(BF), g[:, sl]))
    return [jnp.concatenate(t, axis=1) for t in (dqs, dks, dvs)]


def self_backward_kernel(ok_ref, cos_ref, up_ref, down_ref, q_ref, k_ref, v_ref, g_ref, o_ref):
    cos, up, down = (r[...].reshape(-1, PAIR) for r in (cos_ref, up_ref, down_ref))
    dq, dk, dv = pair_back(flat(q_ref), flat(k_ref), flat(v_ref), flat(g_ref), ok_ref[0])
    dq = turn(dq, cos, -up, -down)
    dk = turn(dk, cos, -up, -down)
    pairs = o_ref.shape[3] // (3 * PAIR)
    hp = pl.program_id(1)
    shape = o_ref.shape[:3] + (PAIR,)
    for which, value in enumerate((dq, dk, dv)):
        at = pl.ds(pl.multiple_of((which * pairs + hp) * PAIR, PAIR), PAIR)
        o_ref[:, :, :, at] = value.astype(BF).reshape(shape)


def cross_forward_kernel(ok_ref, q_ref, k_ref, v_ref, o_ref):
    q, k, v = flat(q_ref), flat(k_ref), flat(v_ref)
    ok = ok_ref[0]
    outs = []
    for h in (0, 1):
        sl = slice(h * HEAD, (h + 1) * HEAD)
        p = soft(q[:, sl], k[:, sl], ok).astype(BF)
        outs.append(mm(p, v[:, sl]))
    o_ref[...] = jnp.concatenate(outs, axis=1).astype(BF).reshape(o_ref.shape)


def cross_backward_kernel(ok_ref, q_ref, k_ref, v_ref, g_ref, dq_ref, dkv_ref):
    dq, dk, dv = pair_back(flat(q_ref), flat(k_ref), flat(v_ref), flat(g_ref), ok_ref[0])
    dq_ref[...] = dq.astype(BF).reshape(dq_ref.shape)
    pairs = dkv_ref.shape[3] // (2 * PAIR)
    hp = pl.program_id(1)
    shape = dkv_ref.shape[:3] + (PAIR,)
    for which, value in enumerate((dk, dv)):
        at = pl.ds(pl.multiple_of((which * pairs + hp) * PAIR, PAIR), PAIR)
        dkv_ref[:, :, :, at] = value.astype(BF).reshape(shape)


def pair_spec(x, offset=0):
    r, _, t, _ = x.shape
    return pl.BlockSpec((r, 1, t, PAIR), lambda b, hp: (0, b, 0, offset + hp))


def wide_spec(r, t, width):
    return pl.BlockSpec((r, 1, t, width), lambda b, hp: (0, b, 0, 0))


def ok_spec(ok):
    return pl.BlockSpec((1, 1, ok.shape[2]), lambda b, hp: (b, 0, 0))


def table_spec(table):
    return pl.BlockSpec(table.shape, lambda b, hp: (0, 0, 0))


def cost(x, keys, products):
    r, b, t, width = x.shape
    return pl.CostEstimate(
        flops=2 * r * b * t * width * keys * products * 2,
        bytes_accessed=8 * x.size,
        transcendentals=r * b * t * keys * (width // HEAD),
    )


def self_forward(ok, tables, qkv):
    r, b, t, width = qkv.shape
    pairs = width // (3 * PAIR)
    shape = jax.ShapeDtypeStruct((r, b, t, pairs * PAIR), BF)
    return pl.pallas_call(
        self_forward_kernel,
        grid=(b, pairs),
        in_specs=[ok_spec(ok)]
        + [table_spec(x) for x in tables]
        + [pair_spec(qkv, i * pairs) for i in range(3)],
        out_specs=[pair_spec(shape)] * 4,
        out_shape=[shape] * 4,
        cost_estimate=cost(shape, r * t, 2),
        name="self_forward",
    )(ok, *tables, qkv, qkv, qkv)


def self_backward(ok, tables, q, k, v, g):
    r, b, t, width = q.shape
    pairs = width // PAIR
    return pl.pallas_call(
        self_backward_kernel,
        grid=(b, pairs),
        in_specs=[ok_spec(ok)] + [table_spec(x) for x in tables] + [pair_spec(q)] * 4,
        out_specs=wide_spec(r, t, 3 * width),
        out_shape=jax.ShapeDtypeStruct((r, b, t, 3 * width), BF),
        cost_estimate=cost(q, r * t, 5),
        name="self_backward",
    )(ok, *tables, q, k, v, g)


def cross_forward(ok, q, kv):
    r, b, t, width = q.shape
    pairs = width // PAIR
    return pl.pallas_call(
        cross_forward_kernel,
        grid=(b, pairs),
        in_specs=[ok_spec(ok), pair_spec(q), pair_spec(kv), pair_spec(kv, pairs)],
        out_specs=pair_spec(q),
        out_shape=jax.ShapeDtypeStruct(q.shape, BF),
        cost_estimate=cost(q, r * kv.shape[2], 2),
        name="cross_forward",
    )(ok, q, kv, kv)


def cross_backward(ok, q, kv, g):
    r, b, t, width = q.shape
    pairs = width // PAIR
    return pl.pallas_call(
        cross_backward_kernel,
        grid=(b, pairs),
        in_specs=[ok_spec(ok), pair_spec(q), pair_spec(kv), pair_spec(kv, pairs), pair_spec(q)],
        out_specs=[pair_spec(q), wide_spec(r, kv.shape[2], kv.shape[3])],
        out_shape=[jax.ShapeDtypeStruct(q.shape, BF), jax.ShapeDtypeStruct(kv.shape, BF)],
        cost_estimate=cost(q, r * kv.shape[2], 5),
        name="cross_backward",
    )(ok, q, kv, kv, g)


def per_device(
    inputs,
    conditioning,
    seq_lengths,
    cond_lengths,
    gain_self,
    gain_cross,
    gain_mlp,
    w_query,
    w_key,
    w_value,
    w_output,
    c_query,
    c_key,
    c_value,
    c_output,
    w_gate,
    w_up,
    w_down,
    cotangent,
):
    batch, tokens_dev, width = inputs.shape
    cond_dev = conditioning.shape[1]
    n = lax.axis_size("seq")
    dp = lax.axis_size("dp")
    s = lax.axis_index("seq")
    d = lax.axis_index("dp")
    rel = jnp.arange(n) ^ s
    mine = width // n

    positions = rel[:, None] * tokens_dev + jnp.arange(tokens_dev)[None, :]
    key_ok = (positions.reshape(1, 1, -1) < seq_lengths[:, None, None]).astype(F32)
    cond_pos = rel[:, None] * cond_dev + jnp.arange(cond_dev)[None, :]
    cond_ok = (cond_pos.reshape(1, 1, -1) < cond_lengths[:, None, None]).astype(F32)
    half = ROT // 2
    inverse = 10000.0 ** (-jnp.arange(half).astype(F32) / half)
    angles = positions.astype(F32)[:, :, None] * inverse
    cosine, sine = jnp.cos(angles), jnp.sin(angles)
    one, nil = jnp.ones(cosine.shape[:2] + (HEAD - ROT,), F32), jnp.zeros_like(cosine)
    nil_rest = jnp.zeros_like(one)
    tables = [
        jnp.concatenate(parts + parts, axis=-1)
        for parts in (
            [cosine, cosine, one],
            [-sine, nil, nil_rest],
            [nil, sine, nil_rest],
        )
    ]

    gain_rows = jnp.stack([gain_self, gain_cross, gain_mlp]).astype(F32)
    share = gain_rows.shape[1]
    gains = all_sum(
        lax.dynamic_update_slice(jnp.zeros((3, width), F32), gain_rows, (0, (d * n + s) * share))
    )
    gain_one, gain_two, gain_three = gains[0], gains[1], gains[2]

    rows = batch * tokens_dev
    total = n * rows
    qkv_w = gather_dp(
        deal(jnp.concatenate([columns_out(w) for w in (w_query, w_key, w_value)], axis=2))
    )
    out_w = gather_head_rows(jnp.concatenate([w_output, c_output], axis=1))
    w_out, c_out = out_w[:, :width], out_w[:, width:]
    cross_w = gather_dp(
        deal(jnp.concatenate([columns_out(w) for w in (c_query, c_key, c_value)], axis=2))
    )
    cq_w, ckv_w = cross_w[:, :mine], cross_w[:, mine:]
    gu_w = gather_dp(deal(jnp.concatenate([blocks_out(w_gate), blocks_out(w_up)], axis=2)))
    down_w = gather_dp(deal(blocks_out(w_down)))
    hid = down_w.shape[1]

    tokens = inputs.reshape(rows, width)
    incoming = cotangent.reshape(rows, width)
    tokens_all = gather_seq(tokens)
    cond_all = gather_seq(conditioning.reshape(batch * cond_dev, width)).reshape(-1, width)
    incoming_all = gather_seq(incoming).reshape(total, width)

    normed_one = norm_forward(tokens_all.reshape(total, width).astype(F32), gain_one)[2]
    qkv = mm(normed_one, qkv_w).reshape(n, batch, tokens_dev, 3 * mine)
    attended, q_rot, k_rot, v_low = self_forward(key_ok, tables, qkv)
    attended = attended.reshape(total, mine)
    partial = mm(attended, w_out).astype(BF).reshape(n, rows, width)
    after_self = tokens.astype(F32) + scatter_seq(partial)
    normal_two, inv_two, own_two = norm_forward(after_self, gain_two)
    normed_two = gather_seq(own_two).reshape(total, width)
    cq = mm(normed_two, cq_w).astype(BF).reshape(n, batch, tokens_dev, mine)
    ckv = mm(cond_all, ckv_w).astype(BF).reshape(n, batch, cond_dev, 2 * mine)
    cross_att = cross_forward(cond_ok, cq, ckv).reshape(total, mine)
    partial = mm(cross_att, c_out).astype(BF).reshape(n, rows, width)
    after_cross = after_self + scatter_seq(partial)
    normal_three, inv_three, own_three = norm_forward(after_cross, gain_three)
    normed_three = gather_seq(own_three).reshape(total, width)
    gate = mm(normed_three, gu_w[:, :hid])
    up = mm(normed_three, gu_w[:, hid:])
    sig = jax.nn.sigmoid(gate)
    hidden = (gate * sig * up).astype(BF)
    partial = mm_t(hidden, down_w).astype(BF).reshape(n, rows, width)
    block = (after_cross + scatter_seq(partial)).astype(BF)
    d_down = t_mm(incoming_all, hidden).astype(BF)
    d_hidden = mm(incoming_all, down_w)
    d_gate = (d_hidden * up * sig * (1.0 + gate * (1.0 - sig))).astype(BF)
    d_up = (d_hidden * gate * sig).astype(BF)
    d_gu = jnp.concatenate([d_gate, d_up], axis=1)
    partial = mm_t(d_gu, gu_w).astype(BF).reshape(n, rows, width)
    d_norm3 = scatter_seq(partial)
    grad_gu = t_mm(normed_three, d_gu).astype(BF)
    back, gain_grad_three = norm_backward(d_norm3, normal_three, inv_three, gain_three)
    d_after_cross = incoming.astype(F32) + back
    dc_low = gather_seq(d_after_cross.astype(BF)).reshape(total, width)
    d_catt = mm_t(dc_low, c_out).astype(BF).reshape(n, batch, tokens_dev, mine)
    grad_c_out = t_mm(cross_att, dc_low).astype(BF)
    d_cq, d_ckv = cross_backward(cond_ok, cq, ckv, d_catt)
    d_cq = d_cq.reshape(total, mine)
    d_ckv = d_ckv.reshape(n * batch * cond_dev, 2 * mine)
    partial = mm_t(d_cq, cq_w).astype(BF).reshape(n, rows, width)
    d_norm2 = scatter_seq(partial)
    partial = mm_t(d_ckv, ckv_w).astype(BF).reshape(n, batch * cond_dev, width)
    grad_cond = scatter_seq(partial)
    grad_cross = jnp.concatenate([t_mm(normed_two, d_cq), t_mm(cond_all, d_ckv)], axis=1).astype(BF)
    back, gain_grad_two = norm_backward(d_norm2, normal_two, inv_two, gain_two)
    d_after_self = d_after_cross + back
    ds_low = gather_seq(d_after_self.astype(BF)).reshape(total, width)
    d_att = mm_t(ds_low, w_out).astype(BF).reshape(n, batch, tokens_dev, mine)
    grad_out = t_mm(attended, ds_low).astype(BF)
    d_qkv = self_backward(key_ok, tables, q_rot, k_rot, v_low, d_att).reshape(total, 3 * mine)
    partial = mm_t(d_qkv, qkv_w).astype(BF).reshape(n, rows, width)
    d_norm1 = scatter_seq(partial)
    grad_qkv = t_mm(normed_one, d_qkv).astype(BF)
    normal_one, inv_one, _ = norm_forward(tokens.astype(F32), gain_one)
    back, gain_grad_one = norm_backward(d_norm1, normal_one, inv_one, gain_one)
    grad_in = d_after_self + back

    def owned(grad):
        return collect(reduce_dp(grad.reshape(dp, width // dp, grad.shape[1])).astype(BF))

    own_down = blocks_back(owned(d_down))
    own_gu = owned(grad_gu)
    own_gate, own_up = blocks_back(own_gu[:, :, :hid]), blocks_back(own_gu[:, :, hid:])
    own_cross = owned(grad_cross)
    own_out = reduce_head_rows(jnp.concatenate([grad_out, grad_c_out], axis=1))
    own_qkv = owned(grad_qkv)
    g_q, g_k, g_v = (columns_back(own_qkv[:, :, i * mine : (i + 1) * mine]) for i in range(3))
    g_cq, g_ck, g_cv = (columns_back(own_cross[:, :, i * mine : (i + 1) * mine]) for i in range(3))
    gain_grads = all_sum(jnp.stack([gain_grad_one, gain_grad_two, gain_grad_three]))
    gain_grads = lax.dynamic_slice(gain_grads, (0, (d * n + s) * share), (3, share))

    def f32(x):
        return x.astype(F32)

    return (
        block.reshape(inputs.shape),
        grad_in.reshape(inputs.shape),
        grad_cond.reshape(conditioning.shape),
        gain_grads[0],
        gain_grads[1],
        gain_grads[2],
        f32(g_q),
        f32(g_k),
        f32(g_v),
        f32(own_out[:, :width]),
        f32(g_cq),
        f32(g_ck),
        f32(g_cv),
        f32(own_out[:, width:]),
        f32(own_gate),
        f32(own_up),
        f32(own_down),
    )


def solution(mesh):
    rows = P("dp", "seq", None)
    split = P(("dp", "seq"))
    matrix = P(("dp", "seq"), None)
    return jax.shard_map(
        per_device,
        mesh=mesh,
        in_specs=(rows, rows, P("dp"), P("dp"), split, split, split) + (matrix,) * 11 + (rows,),
        out_specs=(rows, rows, rows, split, split, split) + (matrix,) * 11,
        check_vma=False,
    )
```

```python
import functools
import math

import jax
import jax.numpy as jnp
from jax import lax
from jax.experimental import pallas as pl
from jax.experimental.pallas import tpu as pltpu
from jax.sharding import PartitionSpec as P

HEADS = 24
HEAD = 64
ROT = 32
EPSILON = 1e-05
BF = jnp.bfloat16
F32 = jnp.float32
PAIR = 2 * HEAD


def mm(left, right):
    return jnp.dot(left, right, preferred_element_type=F32)


def mm_t(left, right):
    return lax.dot_general(left, right, (((1,), (1,)), ((), ())), preferred_element_type=F32)


def t_mm(left, right):
    return lax.dot_general(left, right, (((0,), (0,)), ((), ())), preferred_element_type=F32)


def seq_swap(x, mask):
    n = lax.axis_size("seq")
    return lax.ppermute(x, "seq", [(i, i ^ mask) for i in range(n)])


def dp_swap(x, mask):
    n = lax.axis_size("dp")
    return lax.ppermute(x, "dp", [(i, i ^ mask) for i in range(n)])


def all_sum(v):
    for mask in (1, 2):
        v = v + seq_swap(v, mask)
    mask = 1
    while mask < lax.axis_size("dp"):
        v = v + dp_swap(v, mask)
        mask *= 2
    return v


def gather_seq(x):
    core = seq_swap(x, 1)
    far = seq_swap(x, 2)
    diag = seq_swap(far, 1)
    return jnp.stack([x, core, far, diag])


def scatter_seq(partial):
    far = partial[2].astype(F32) + seq_swap(partial[3], 1).astype(F32)
    arrived = seq_swap(far.astype(BF), 2)
    near = partial[0].astype(F32) + seq_swap(partial[1], 1).astype(F32)
    return near + arrived.astype(F32)


def x_swap(x):
    return dp_swap(x, 1)


def gather_eight(x):
    half = x.shape[0] // 2
    far = seq_swap(x, 2)
    side = x_swap(x)
    corner = jnp.concatenate([x_swap(far[:half]), seq_swap(side[half:], 2)])
    blocks = []
    for near in (x, far, side, corner):
        blocks += [near, seq_swap(near, 1)]
    return jnp.stack(blocks)


def scatter_eight(partial):
    half = partial.shape[1] // 2

    def with_core(k):
        return partial[k].astype(F32) + seq_swap(partial[k + 1], 1).astype(F32)

    corner = with_core(6).astype(BF)
    from_x, from_y = x_swap(corner[:half]), seq_swap(corner[half:], 2)
    far = with_core(2)
    far = jnp.concatenate([far[:half] + from_x.astype(F32), far[half:]]).astype(BF)
    side = with_core(4)
    side = jnp.concatenate([side[:half], side[half:] + from_y.astype(F32)]).astype(BF)
    from_y, from_x = seq_swap(far, 2), x_swap(side)
    return with_core(0) + from_y.astype(F32) + from_x.astype(F32)


def together(*values):
    return lax.optimization_barrier(values)


RING_Z, RING_X = 4, 2


def ringed():
    return lax.axis_size("dp") == RING_Z * RING_X


def z_groups():
    return [[z * RING_X + x for z in range(RING_Z)] for x in range(RING_X)]


def gather_z(chunk):
    return lax.all_gather(chunk, "dp", axis=0, axis_index_groups=z_groups())


def gather_dp(chunk):
    if not ringed():
        return lax.all_gather(chunk, "dp", axis=0, tiled=True)
    rows, cols = chunk.shape
    first = lax.axis_index("dp") % RING_X == 0
    own = gather_z(chunk)
    other = dp_swap(own, 1)
    both = jnp.stack([jnp.where(first, own, other), jnp.where(first, other, own)], axis=1)
    return both.reshape(-1, cols)


def reduce_dp(slots):
    n, rows, cols = slots.shape
    if not ringed():
        return lax.psum_scatter(
            slots.reshape(n * rows, cols), "dp", scatter_dimension=0, tiled=True
        )
    xx = lax.axis_index("dp") % RING_X
    split = slots.reshape(RING_Z, RING_X, rows, cols)
    away = lax.dynamic_index_in_dim(split, 1 - xx, axis=1, keepdims=False)
    kept = lax.dynamic_index_in_dim(split, xx, axis=1, keepdims=False)
    arrived = dp_swap(away, 1)
    both = (kept.astype(F32) + arrived.astype(F32)).astype(BF)
    return lax.psum_scatter(
        both.reshape(RING_Z * rows, cols),
        "dp",
        scatter_dimension=0,
        tiled=True,
        axis_index_groups=z_groups(),
    )


def wide():
    return lax.axis_size("seq") * (RING_X if ringed() else 1)


def hidden_out(mats):
    n = lax.axis_size("seq")
    parts = wide() // n
    rows = mats[0].shape[0]
    cut = [m.reshape(rows, n, parts, -1) for m in mats]
    return jnp.concatenate(cut, axis=3).transpose(1, 0, 2, 3).reshape(n, rows, -1)


def deal_hidden(x):
    got = deal(x)
    if not ringed():
        return got
    rows = got.shape[0]
    xx = lax.axis_index("dp") % RING_X
    cut = got.reshape(rows, RING_X, -1)
    kept = lax.dynamic_index_in_dim(cut, xx, 1, keepdims=False)
    arrived = x_swap(lax.dynamic_index_in_dim(cut, 1 - xx, 1, keepdims=False))
    first = xx == 0
    return jnp.concatenate([jnp.where(first, kept, arrived), jnp.where(first, arrived, kept)])


def gather_hidden(x):
    if not ringed():
        return lax.all_gather(x, "dp", axis=0, tiled=True)
    return lax.all_gather(x, "dp", axis=0, tiled=True, axis_index_groups=z_groups())


def reduce_hidden(grad):
    if not ringed():
        return lax.psum_scatter(grad, "dp", scatter_dimension=0, tiled=True)
    return lax.psum_scatter(
        grad, "dp", scatter_dimension=0, tiled=True, axis_index_groups=z_groups()
    )


def collect_hidden(x, count):
    n = lax.axis_size("seq")
    parts = wide() // n
    if ringed():
        xx = lax.axis_index("dp") % RING_X
        cut = x.reshape(RING_X, -1, x.shape[1])
        kept = lax.dynamic_index_in_dim(cut, xx, 0, keepdims=False)
        arrived = x_swap(lax.dynamic_index_in_dim(cut, 1 - xx, 0, keepdims=False))
        first = xx == 0
        x = jnp.concatenate(
            [jnp.where(first, kept, arrived), jnp.where(first, arrived, kept)], axis=1
        )
    got = collect(x)
    rows = got.shape[1]
    got = got.reshape(n, rows, parts, count, -1)
    return [got[:, :, :, i].transpose(1, 0, 2, 3).reshape(rows, -1) for i in range(count)]


def columns_out(x):
    rows = x.shape[0]
    n = lax.axis_size("seq")
    return x.reshape(rows, HEADS // n, n, HEAD).transpose(2, 0, 1, 3).reshape(n, rows, -1)


def columns_back(x):
    n, rows, _ = x.shape
    return x.reshape(n, rows, HEADS // n, HEAD).transpose(1, 2, 0, 3).reshape(rows, HEADS * HEAD)


def deal(x):
    got = lax.all_to_all(x, "seq", split_axis=0, concat_axis=0, tiled=True)
    return got.reshape(-1, x.shape[-1])


def collect(x):
    n = lax.axis_size("seq")
    return lax.all_to_all(
        x.reshape(n, -1, x.shape[-1]), "seq", split_axis=0, concat_axis=0, tiled=True
    )


def head_slot():
    s, d = lax.axis_index("seq"), lax.axis_index("dp")
    n = lax.axis_size("seq")
    per = HEADS // lax.axis_size("dp")
    return (s + (n - per % n) * d) % n, per, n


def slot_place(d):
    s = lax.axis_index("seq")
    n = lax.axis_size("seq")
    per = HEADS // lax.axis_size("dp")
    j = (s + (n - per % n) * d) % n
    return jnp.where(j < per, (per * d + j - s) // n, HEADS // n)


def gather_head_rows(x):
    n = lax.axis_size("seq")
    s = lax.axis_index("seq")
    cols = x.shape[1]
    mine = HEADS // n
    if not ringed():
        full = lax.all_gather(x, ("dp", "seq"), axis=0, tiled=True)
        picked = lax.dynamic_index_in_dim(full.reshape(mine, n, HEAD, cols), s, 1, keepdims=False)
        return picked.reshape(mine * HEAD, cols)
    rows = lax.all_gather(x, "seq", axis=0, tiled=True)
    j, per, _ = head_slot()
    rows = jnp.concatenate([rows, jnp.zeros((HEAD, cols), x.dtype)])
    piece = lax.dynamic_slice(rows, (j * HEAD, 0), (HEAD, cols))
    out = jnp.zeros(((mine + 1) * HEAD, cols), x.dtype)
    own = gather_z(piece)
    other = dp_swap(own, 1)
    xx = lax.axis_index("dp") % RING_X
    for z in range(RING_Z):
        for held, x_of in ((own, xx), (other, 1 - xx)):
            place = slot_place(z * RING_X + x_of) * HEAD
            out = lax.dynamic_update_slice(out, held[z], (place, 0))
    return out[: mine * HEAD]


def reduce_head_rows(x):
    n = lax.axis_size("seq")
    s = lax.axis_index("seq")
    size = lax.axis_size("dp")
    cols = x.shape[1]
    mine = HEADS // n
    if not ringed():
        full = jnp.zeros((mine, n, HEAD, cols), BF)
        full = lax.dynamic_update_index_in_dim(full, x.reshape(mine, 1, HEAD, cols), s, 1)
        return lax.psum_scatter(
            full.reshape(-1, cols), ("dp", "seq"), scatter_dimension=0, tiled=True
        ).astype(F32)
    padded = jnp.concatenate([x, jnp.zeros((HEAD, cols), x.dtype)])
    slots = jnp.stack(
        [lax.dynamic_slice(padded, (slot_place(d) * HEAD, 0), (HEAD, cols)) for d in range(size)]
    )
    own = reduce_dp(slots)
    pieces = lax.all_gather(own, "seq", axis=0, tiled=False)
    per = HEADS // size
    d = lax.axis_index("dp")
    rows = jnp.concatenate(
        [
            lax.dynamic_index_in_dim(pieces, (per * d + j) % n, 0, keepdims=False)
            for j in range(per)
        ]
    )
    share = per * HEAD // n
    return lax.dynamic_slice(rows, (s * share, 0), (share, cols)).astype(F32)


def norm_forward(values, gain_vec):
    average = jnp.mean(values, axis=-1, keepdims=True)
    centred = values - average
    variance = jnp.mean(centred * centred, axis=-1, keepdims=True)
    inv_std = lax.rsqrt(variance + EPSILON)
    normal = centred * inv_std
    return normal, inv_std, (normal * gain_vec).astype(BF)


def norm_backward(grad_normed, normal, inv_std, gain_vec):
    grad_gain = jnp.sum(grad_normed * normal, axis=0)
    grad_hat = grad_normed * gain_vec
    mean_hat = jnp.mean(grad_hat, axis=-1, keepdims=True)
    mean_mix = jnp.mean(grad_hat * normal, axis=-1, keepdims=True)
    return inv_std * (grad_hat - mean_hat - normal * mean_mix), grad_gain


def flat(ref):
    value = ref[...]
    return value.reshape(value.shape[0] * value.shape[1] * value.shape[2], value.shape[3])


def turn(m, cos, up, down):
    return m * cos + pltpu.roll(m, PAIR - ROT // 2, 1) * up + pltpu.roll(m, ROT // 2, 1) * down


SCALE = 1.0 / math.sqrt(HEAD)


def soft(q, k, ok):
    scores = mm_t(q, k) * SCALE
    scores = jnp.where(ok > 0.0, scores, -1e30)
    top = jnp.max(scores, axis=-1, keepdims=True)
    e = jnp.exp(scores - top)
    return e * (1.0 / jnp.sum(e, axis=-1, keepdims=True))


def self_forward_kernel(ok_ref, cos_ref, up_ref, down_ref, q_ref, k_ref, v_ref, o_ref, qr_ref, kr_ref, vr_ref):
    cos, up, down = (r[...].reshape(-1, PAIR) for r in (cos_ref, up_ref, down_ref))
    q = turn(flat(q_ref), cos, up, down).astype(BF)
    k = turn(flat(k_ref), cos, up, down).astype(BF)
    v = flat(v_ref).astype(BF)
    ok = ok_ref[0]
    outs = []
    for h in (0, 1):
        sl = slice(h * HEAD, (h + 1) * HEAD)
        p = soft(q[:, sl], k[:, sl], ok).astype(BF)
        outs.append(mm(p, v[:, sl]))
    o_ref[...] = jnp.concatenate(outs, axis=1).astype(BF).reshape(o_ref.shape)
    qr_ref[...] = q.reshape(qr_ref.shape)
    kr_ref[...] = k.reshape(kr_ref.shape)
    vr_ref[...] = v.reshape(vr_ref.shape)


def pair_back(q, k, v, g, ok):
    dqs, dks, dvs = [], [], []
    for h in (0, 1):
        sl = slice(h * HEAD, (h + 1) * HEAD)
        p = soft(q[:, sl], k[:, sl], ok)
        dp = mm_t(g[:, sl], v[:, sl])
        inner = jnp.sum(p * dp, axis=-1, keepdims=True)
        ds = (p * (dp - inner)).astype(BF)
        dqs.append(mm(ds, k[:, sl]) * SCALE)
        dks.append(t_mm(ds, q[:, sl]) * SCALE)
        dvs.append(t_mm(p.astype(BF), g[:, sl]))
    return [jnp.concatenate(t, axis=1) for t in (dqs, dks, dvs)]


def self_backward_kernel(ok_ref, cos_ref, up_ref, down_ref, q_ref, k_ref, v_ref, g_ref, o_ref):
    cos, up, down = (r[...].reshape(-1, PAIR) for r in (cos_ref, up_ref, down_ref))
    dq, dk, dv = pair_back(flat(q_ref), flat(k_ref), flat(v_ref), flat(g_ref), ok_ref[0])
    dq = turn(dq, cos, -up, -down)
    dk = turn(dk, cos, -up, -down)
    pairs = o_ref.shape[3] // (3 * PAIR)
    hp = pl.program_id(1)
    shape = o_ref.shape[:3] + (PAIR,)
    for which, value in enumerate((dq, dk, dv)):
        at = pl.ds(pl.multiple_of((which * pairs + hp) * PAIR, PAIR), PAIR)
        o_ref[:, :, :, at] = value.astype(BF).reshape(shape)


def cross_forward_kernel(ok_ref, q_ref, k_ref, v_ref, o_ref):
    q, k, v = flat(q_ref), flat(k_ref), flat(v_ref)
    ok = ok_ref[0]
    outs = []
    for h in (0, 1):
        sl = slice(h * HEAD, (h + 1) * HEAD)
        p = soft(q[:, sl], k[:, sl], ok).astype(BF)
        outs.append(mm(p, v[:, sl]))
    o_ref[...] = jnp.concatenate(outs, axis=1).astype(BF).reshape(o_ref.shape)


def cross_backward_kernel(ok_ref, q_ref, k_ref, v_ref, g_ref, dq_ref, dkv_ref):
    dq, dk, dv = pair_back(flat(q_ref), flat(k_ref), flat(v_ref), flat(g_ref), ok_ref[0])
    dq_ref[...] = dq.astype(BF).reshape(dq_ref.shape)
    pairs = dkv_ref.shape[3] // (2 * PAIR)
    hp = pl.program_id(1)
    shape = dkv_ref.shape[:3] + (PAIR,)
    for which, value in enumerate((dk, dv)):
        at = pl.ds(pl.multiple_of((which * pairs + hp) * PAIR, PAIR), PAIR)
        dkv_ref[:, :, :, at] = value.astype(BF).reshape(shape)


def pair_spec(x, offset=0):
    r, _, t, _ = x.shape
    return pl.BlockSpec((r, 1, t, PAIR), lambda b, hp: (0, b, 0, offset + hp))


def wide_spec(r, t, width):
    return pl.BlockSpec((r, 1, t, width), lambda b, hp: (0, b, 0, 0))


def ok_spec(ok):
    return pl.BlockSpec((1, 1, ok.shape[2]), lambda b, hp: (b, 0, 0))


def table_spec(table):
    return pl.BlockSpec(table.shape, lambda b, hp: (0, 0, 0))


def cost(x, keys, products):
    r, b, t, width = x.shape
    return pl.CostEstimate(
        flops=2 * r * b * t * width * keys * products * 2,
        bytes_accessed=8 * x.size,
        transcendentals=r * b * t * keys * (width // HEAD),
    )


def self_forward(ok, tables, qkv):
    r, b, t, width = qkv.shape
    pairs = width // (3 * PAIR)
    shape = jax.ShapeDtypeStruct((r, b, t, pairs * PAIR), BF)
    return pl.pallas_call(
        self_forward_kernel,
        grid=(b, pairs),
        in_specs=[ok_spec(ok)]
        + [table_spec(x) for x in tables]
        + [pair_spec(qkv, i * pairs) for i in range(3)],
        out_specs=[pair_spec(shape)] * 4,
        out_shape=[shape] * 4,
        cost_estimate=cost(shape, r * t, 2),
        name="self_forward",
    )(ok, *tables, qkv, qkv, qkv)


def self_backward(ok, tables, q, k, v, g):
    r, b, t, width = q.shape
    pairs = width // PAIR
    return pl.pallas_call(
        self_backward_kernel,
        grid=(b, pairs),
        in_specs=[ok_spec(ok)] + [table_spec(x) for x in tables] + [pair_spec(q)] * 4,
        out_specs=wide_spec(r, t, 3 * width),
        out_shape=jax.ShapeDtypeStruct((r, b, t, 3 * width), BF),
        cost_estimate=cost(q, r * t, 5),
        name="self_backward",
    )(ok, *tables, q, k, v, g)


def cross_forward(ok, q, kv):
    r, b, t, width = q.shape
    pairs = width // PAIR
    return pl.pallas_call(
        cross_forward_kernel,
        grid=(b, pairs),
        in_specs=[ok_spec(ok), pair_spec(q), pair_spec(kv), pair_spec(kv, pairs)],
        out_specs=pair_spec(q),
        out_shape=jax.ShapeDtypeStruct(q.shape, BF),
        cost_estimate=cost(q, r * kv.shape[2], 2),
        name="cross_forward",
    )(ok, q, kv, kv)


def cross_backward(ok, q, kv, g):
    r, b, t, width = q.shape
    pairs = width // PAIR
    return pl.pallas_call(
        cross_backward_kernel,
        grid=(b, pairs),
        in_specs=[ok_spec(ok), pair_spec(q), pair_spec(kv), pair_spec(kv, pairs), pair_spec(q)],
        out_specs=[pair_spec(q), wide_spec(r, kv.shape[2], kv.shape[3])],
        out_shape=[jax.ShapeDtypeStruct(q.shape, BF), jax.ShapeDtypeStruct(kv.shape, BF)],
        cost_estimate=cost(q, r * kv.shape[2], 5),
        name="cross_backward",
    )(ok, q, kv, kv, g)


def per_device(
    inputs,
    conditioning,
    seq_lengths,
    cond_lengths,
    gain_self,
    gain_cross,
    gain_mlp,
    w_query,
    w_key,
    w_value,
    w_output,
    c_query,
    c_key,
    c_value,
    c_output,
    w_gate,
    w_up,
    w_down,
    cotangent,
):
    batch, tokens_dev, width = inputs.shape
    cond_dev = conditioning.shape[1]
    n = lax.axis_size("seq")
    dp = lax.axis_size("dp")
    s = lax.axis_index("seq")
    d = lax.axis_index("dp")
    rel = jnp.arange(n) ^ s
    mine = width // n

    positions = rel[:, None] * tokens_dev + jnp.arange(tokens_dev)[None, :]
    key_ok = (positions.reshape(1, 1, -1) < seq_lengths[:, None, None]).astype(F32)
    cond_pos = rel[:, None] * cond_dev + jnp.arange(cond_dev)[None, :]
    cond_ok = (cond_pos.reshape(1, 1, -1) < cond_lengths[:, None, None]).astype(F32)
    half = ROT // 2
    inverse = 10000.0 ** (-jnp.arange(half).astype(F32) / half)
    angles = positions.astype(F32)[:, :, None] * inverse
    cosine, sine = jnp.cos(angles), jnp.sin(angles)
    one, nil = jnp.ones(cosine.shape[:2] + (HEAD - ROT,), F32), jnp.zeros_like(cosine)
    nil_rest = jnp.zeros_like(one)
    tables = [
        jnp.concatenate(parts + parts, axis=-1)
        for parts in (
            [cosine, cosine, one],
            [-sine, nil, nil_rest],
            [nil, sine, nil_rest],
        )
    ]

    gain_rows = jnp.stack([gain_self, gain_cross, gain_mlp]).astype(F32)
    share = gain_rows.shape[1]
    gains = all_sum(
        lax.dynamic_update_slice(jnp.zeros((3, width), F32), gain_rows, (0, (d * n + s) * share))
    )
    gain_one, gain_two, gain_three = gains[0], gains[1], gains[2]

    rows = batch * tokens_dev
    total = n * rows
    qkv_w = gather_dp(
        deal(jnp.concatenate([columns_out(w) for w in (w_query, w_key, w_value)], axis=2))
    )
    out_w = gather_head_rows(jnp.concatenate([w_output, c_output], axis=1))
    w_out, c_out = out_w[:, :width], out_w[:, width:]
    cross_w = gather_dp(
        deal(jnp.concatenate([columns_out(w) for w in (c_query, c_key, c_value)], axis=2))
    )
    cq_w, ckv_w = cross_w[:, :mine], cross_w[:, mine:]
    ffn_w = deal_hidden(hidden_out([w_gate, w_up, w_down]))
    hid = w_gate.shape[1] // wide()
    gu_w = gather_hidden(ffn_w[:, : 2 * hid])
    down_w = gather_hidden(ffn_w[:, 2 * hid :])
    gather_ffn, scatter_ffn = (
        (gather_eight, scatter_eight) if ringed() else (gather_seq, scatter_seq)
    )
    shared = wide()

    tokens = inputs.reshape(rows, width)
    incoming = cotangent.reshape(rows, width)
    tokens_all = gather_seq(tokens)
    cond_all = gather_seq(conditioning.reshape(batch * cond_dev, width)).reshape(-1, width)
    incoming_all = gather_ffn(incoming).reshape(shared * rows, width)

    normed_one = norm_forward(tokens_all.reshape(total, width).astype(F32), gain_one)[2]
    qkv = mm(normed_one, qkv_w).reshape(n, batch, tokens_dev, 3 * mine)
    attended, q_rot, k_rot, v_low = self_forward(key_ok, tables, qkv)
    attended = attended.reshape(total, mine)
    partial = mm(attended, w_out).astype(BF).reshape(n, rows, width)
    after_self = tokens.astype(F32) + scatter_seq(partial)
    normal_two, inv_two, own_two = norm_forward(after_self, gain_two)
    normed_two = gather_seq(own_two).reshape(total, width)
    cq = mm(normed_two, cq_w).astype(BF).reshape(n, batch, tokens_dev, mine)
    ckv = mm(cond_all, ckv_w).astype(BF).reshape(n, batch, cond_dev, 2 * mine)
    cross_att = cross_forward(cond_ok, cq, ckv).reshape(total, mine)
    partial = mm(cross_att, c_out).astype(BF).reshape(n, rows, width)
    after_cross = after_self + scatter_seq(partial)
    normal_three, inv_three, own_three = norm_forward(after_cross, gain_three)
    normed_three = gather_ffn(own_three).reshape(shared * rows, width)
    gate = mm(normed_three, gu_w[:, :hid])
    up = mm(normed_three, gu_w[:, hid:])
    sig = jax.nn.sigmoid(gate)
    hidden = (gate * sig * up).astype(BF)
    grad_down = t_mm(incoming_all, hidden).astype(BF)
    incoming_all, grad_down = together(incoming_all, grad_down)
    d_hidden = mm(incoming_all, down_w)
    d_gate = (d_hidden * up * sig * (1.0 + gate * (1.0 - sig))).astype(BF)
    d_up = (d_hidden * gate * sig).astype(BF)
    d_gu = jnp.concatenate([d_gate, d_up], axis=1)
    partial = mm_t(d_gu, gu_w).astype(BF).reshape(shared, rows, width)
    d_norm3 = scatter_ffn(partial)
    grad_gu = t_mm(normed_three, d_gu).astype(BF)
    d_norm3, grad_gu = together(d_norm3, grad_gu)
    partial = mm_t(hidden, down_w).astype(BF).reshape(shared, rows, width)
    block = (after_cross + scatter_ffn(partial)).astype(BF)
    back, gain_grad_three = norm_backward(d_norm3, normal_three, inv_three, gain_three)
    d_after_cross = incoming.astype(F32) + back
    dc_low = gather_seq(d_after_cross.astype(BF)).reshape(total, width)
    d_catt = mm_t(dc_low, c_out).astype(BF).reshape(n, batch, tokens_dev, mine)
    grad_c_out = t_mm(cross_att, dc_low).astype(BF)
    d_cq, d_ckv = cross_backward(cond_ok, cq, ckv, d_catt)
    d_cq = d_cq.reshape(total, mine)
    d_ckv = d_ckv.reshape(n * batch * cond_dev, 2 * mine)
    partial = mm_t(d_cq, cq_w).astype(BF).reshape(n, rows, width)
    d_norm2 = scatter_seq(partial)
    grad_cross = jnp.concatenate([t_mm(normed_two, d_cq), t_mm(cond_all, d_ckv)], axis=1).astype(BF)
    d_norm2, grad_cross = together(d_norm2, grad_cross)
    partial = mm_t(d_ckv, ckv_w).astype(BF).reshape(n, batch * cond_dev, width)
    grad_cond = scatter_seq(partial)
    back, gain_grad_two = norm_backward(d_norm2, normal_two, inv_two, gain_two)
    d_after_self = d_after_cross + back
    ds_low = gather_seq(d_after_self.astype(BF)).reshape(total, width)
    ds_low, grad_c_out = together(ds_low, grad_c_out)
    d_att = mm_t(ds_low, w_out).astype(BF).reshape(n, batch, tokens_dev, mine)
    grad_out = t_mm(attended, ds_low).astype(BF)
    d_qkv = self_backward(key_ok, tables, q_rot, k_rot, v_low, d_att).reshape(total, 3 * mine)
    grad_qkv = t_mm(normed_one, d_qkv).astype(BF)
    d_qkv, grad_qkv = together(d_qkv, grad_qkv)
    partial = mm_t(d_qkv, qkv_w).astype(BF).reshape(n, rows, width)
    d_norm1 = scatter_seq(partial)
    normal_one, inv_one, _ = norm_forward(tokens.astype(F32), gain_one)
    back, gain_grad_one = norm_backward(d_norm1, normal_one, inv_one, gain_one)
    grad_in = d_after_self + back

    def owned(grad):
        return collect(reduce_dp(grad.reshape(dp, width // dp, grad.shape[1])))

    own_down = reduce_hidden(grad_down)
    own_gu = reduce_hidden(grad_gu)
    own_gate, own_up, own_down = collect_hidden(jnp.concatenate([own_gu, own_down], axis=1), 3)
    own_cross = owned(grad_cross)
    own_out = reduce_head_rows(jnp.concatenate([grad_out, grad_c_out], axis=1))
    own_qkv = owned(grad_qkv)
    g_q, g_k, g_v = (columns_back(own_qkv[:, :, i * mine : (i + 1) * mine]) for i in range(3))
    g_cq, g_ck, g_cv = (columns_back(own_cross[:, :, i * mine : (i + 1) * mine]) for i in range(3))
    gain_grads = all_sum(jnp.stack([gain_grad_one, gain_grad_two, gain_grad_three]))
    gain_grads = lax.dynamic_slice(gain_grads, (0, (d * n + s) * share), (3, share))

    def f32(x):
        return x.astype(F32)

    return (
        block.reshape(inputs.shape),
        grad_in.reshape(inputs.shape),
        grad_cond.reshape(conditioning.shape),
        gain_grads[0],
        gain_grads[1],
        gain_grads[2],
        f32(g_q),
        f32(g_k),
        f32(g_v),
        f32(own_out[:, :width]),
        f32(g_cq),
        f32(g_ck),
        f32(g_cv),
        f32(own_out[:, width:]),
        f32(own_gate),
        f32(own_up),
        f32(own_down),
    )


def solution(mesh):
    rows = P("dp", "seq", None)
    split = P(("dp", "seq"))
    matrix = P(("dp", "seq"), None)
    return jax.shard_map(
        per_device,
        mesh=mesh,
        in_specs=(rows, rows, P("dp"), P("dp"), split, split, split) + (matrix,) * 11 + (rows,),
        out_specs=(rows, rows, rows, split, split, split) + (matrix,) * 11,
        check_vma=False,
    )
```

```python
import functools
import math

import jax
import jax.numpy as jnp
from jax import lax
from jax.experimental import pallas as pl
from jax.experimental.pallas import tpu as pltpu
from jax.sharding import PartitionSpec as P

HEADS = 24
HEAD = 64
ROT = 32
EPSILON = 1e-05
BF = jnp.bfloat16
F32 = jnp.float32
PAIR = 2 * HEAD


def mm(left, right):
    return jnp.dot(left, right, preferred_element_type=F32)


def mm_t(left, right):
    return lax.dot_general(left, right, (((1,), (1,)), ((), ())), preferred_element_type=F32)


def t_mm(left, right):
    return lax.dot_general(left, right, (((0,), (0,)), ((), ())), preferred_element_type=F32)


def seq_swap(x, mask):
    n = lax.axis_size("seq")
    return lax.ppermute(x, "seq", [(i, i ^ mask) for i in range(n)])


def dp_swap(x, mask):
    n = lax.axis_size("dp")
    return lax.ppermute(x, "dp", [(i, i ^ mask) for i in range(n)])


def all_sum_dp(v):
    mask = lax.axis_size("dp") // 2
    while mask:
        v = v + dp_swap(v, mask)
        mask //= 2
    return v


def gather_seq(x, beside=()):
    core = seq_swap(x, 1)
    far = seq_swap(x, 2)
    if beside:
        far, *beside = together(far, *beside)
    diag = seq_swap(far, 1)
    blocks = jnp.stack([x, core, far, diag])
    return (blocks, *beside) if beside else blocks


def scatter_seq(partial, beside=()):
    far = partial[2].astype(F32) + seq_swap(partial[3], 1).astype(F32)
    arrived = seq_swap(far.astype(BF), 2)
    arrived, *beside = together(arrived, *beside)
    near = partial[0].astype(F32) + seq_swap(partial[1], 1).astype(F32)
    total = near + arrived.astype(F32)
    return (total, *beside) if beside else total


def x_swap(x):
    return dp_swap(x, 1)


def all_sum(v):
    for mask in (2, 1):
        v = v + seq_swap(v, mask)
    return all_sum_dp(v)


def natural(blocks):
    s = lax.axis_index("seq")
    n = lax.axis_size("seq")
    return [lax.dynamic_index_in_dim(blocks, k ^ s, 0, keepdims=False) for k in range(n)]


def gather_eight_first(x):
    return x, seq_swap(x, 2), x_swap(x)


def gather_eight(x):
    return gather_eight_last(*gather_eight_first(x))


def gather_eight_last(x, far, side):
    half = x.shape[0] // 2
    corner = jnp.concatenate([x_swap(far[:half]), seq_swap(side[half:], 2)])
    blocks = []
    for near in (x, far, side, corner):
        blocks += [near, seq_swap(near, 1)]
    return jnp.stack(blocks)


def scatter_eight(partial, first=None, second=None):
    half = partial.shape[1] // 2

    def with_core(k):
        return partial[k].astype(F32) + seq_swap(partial[k + 1], 1).astype(F32)

    corner = with_core(6).astype(BF)
    corner, partial = together(corner, partial)
    from_x, from_y = x_swap(corner[:half]), seq_swap(corner[half:], 2)
    out = []
    if first is not None:
        value = first(corner)
        from_x, from_y, value = together(from_x, from_y, value)
        out.append(value)
    far = with_core(2)
    far = jnp.concatenate([far[:half] + from_x.astype(F32), far[half:]]).astype(BF)
    side = with_core(4)
    side = jnp.concatenate([side[:half], side[half:] + from_y.astype(F32)]).astype(BF)
    far, side = together(far, side)
    from_y, from_x = seq_swap(far, 2), x_swap(side)
    if second is not None:
        value = second(far)
        from_y, from_x, value = together(from_y, from_x, value)
        out.append(value)
    return (with_core(0) + from_y.astype(F32) + from_x.astype(F32), *out)


def scatter_eight_x(partial):
    def with_core(k):
        return partial[k].astype(F32) + seq_swap(partial[k + 1], 1).astype(F32)

    away = jnp.stack([with_core(4).astype(BF), with_core(6).astype(BF)])
    arrived = x_swap(away)
    near = with_core(0) + arrived[0].astype(F32)
    return near, (with_core(2) + arrived[1].astype(F32)).astype(BF)


def together(*values):
    return lax.optimization_barrier(values)


RING_Z, RING_X = 4, 2


def ringed():
    return lax.axis_size("dp") == RING_Z * RING_X


def z_groups():
    return [[z * RING_X + x for z in range(RING_Z)] for x in range(RING_X)]


def gather_z(chunk):
    return lax.all_gather(chunk, "dp", axis=0, axis_index_groups=z_groups())


def gather_dp_z(chunk):
    if not ringed():
        return lax.all_gather(chunk, "dp", axis=0, tiled=True)
    return gather_z(chunk)


def pair_x(chunk):
    if not ringed():
        return chunk
    other = x_swap(chunk)
    first = lax.axis_index("dp") % RING_X == 0
    return jnp.concatenate([jnp.where(first, chunk, other), jnp.where(first, other, chunk)])


def gather_dp_x(own, other=None):
    if not ringed():
        return own
    cols = own.shape[2]
    first = lax.axis_index("dp") % RING_X == 0
    other = dp_swap(own, 1) if other is None else other
    both = jnp.stack([jnp.where(first, own, other), jnp.where(first, other, own)], axis=1)
    return both.reshape(-1, cols)


def reduce_dp_x(slots):
    kept, away = split_x(slots)
    return join_x(kept, x_swap(away) if ringed() else None)


def split_x(slots):
    n, rows, cols = slots.shape
    if not ringed():
        return slots, slots
    xx = lax.axis_index("dp") % RING_X
    split = slots.reshape(RING_Z, RING_X, rows, cols)
    away = lax.dynamic_index_in_dim(split, 1 - xx, axis=1, keepdims=False)
    kept = lax.dynamic_index_in_dim(split, xx, axis=1, keepdims=False)
    return kept, away


def join_x(kept, arrived):
    if ringed():
        kept = (kept.astype(F32) + arrived.astype(F32)).astype(BF)
    return kept.reshape(-1, kept.shape[-1])


def reduce_dp_z(both):
    if not ringed():
        return lax.psum_scatter(both, "dp", scatter_dimension=0, tiled=True)
    return lax.psum_scatter(
        both, "dp", scatter_dimension=0, tiled=True, axis_index_groups=z_groups()
    )


def reduce_dp(slots):
    return reduce_dp_z(reduce_dp_x(slots))


def wide():
    return lax.axis_size("seq") * (RING_X if ringed() else 1)


def hidden_out(mats):
    n = lax.axis_size("seq")
    parts = wide() // n
    rows = mats[0].shape[0]
    cut = [m.reshape(rows, n, parts, -1) for m in mats]
    return jnp.concatenate(cut, axis=3).transpose(1, 0, 2, 3).reshape(n, rows, -1)


def deal_hidden_x(got):
    if not ringed():
        return got
    rows = got.shape[0]
    xx = lax.axis_index("dp") % RING_X
    cut = got.reshape(rows, RING_X, -1)
    kept = lax.dynamic_index_in_dim(cut, xx, 1, keepdims=False)
    arrived = x_swap(lax.dynamic_index_in_dim(cut, 1 - xx, 1, keepdims=False))
    first = xx == 0
    return jnp.concatenate([jnp.where(first, kept, arrived), jnp.where(first, arrived, kept)])


def gather_hidden(x):
    if not ringed():
        return lax.all_gather(x, "dp", axis=0, tiled=True)
    return lax.all_gather(x, "dp", axis=0, tiled=True, axis_index_groups=z_groups())


def reduce_hidden(grad):
    if not ringed():
        return lax.psum_scatter(grad, "dp", scatter_dimension=0, tiled=True)
    return lax.psum_scatter(
        grad, "dp", scatter_dimension=0, tiled=True, axis_index_groups=z_groups()
    )


def split_rows(x):
    xx = lax.axis_index("dp") % RING_X
    cut = x.reshape(RING_X, -1, x.shape[1])
    kept = lax.dynamic_index_in_dim(cut, xx, 0, keepdims=False)
    return kept, lax.dynamic_index_in_dim(cut, 1 - xx, 0, keepdims=False)


def join_hidden(kept, arrived):
    first = lax.axis_index("dp") % RING_X == 0
    return jnp.concatenate(
        [jnp.where(first, kept, arrived), jnp.where(first, arrived, kept)], axis=1
    )


def part_hidden(got, count):
    n = lax.axis_size("seq")
    parts = wide() // n
    rows = got.shape[1]
    got = got.reshape(n, rows, parts, count, -1)
    return [got[:, :, :, i].transpose(1, 0, 2, 3).reshape(rows, -1) for i in range(count)]


def columns_out(x):
    rows = x.shape[0]
    n = lax.axis_size("seq")
    return x.reshape(rows, HEADS // n, n, HEAD).transpose(2, 0, 1, 3).reshape(n, rows, -1)


def columns_back(x):
    n, rows, _ = x.shape
    return x.reshape(n, rows, HEADS // n, HEAD).transpose(1, 2, 0, 3).reshape(rows, HEADS * HEAD)


def deal(x):
    got = lax.all_to_all(x, "seq", split_axis=0, concat_axis=0, tiled=True)
    return got.reshape(-1, x.shape[-1])


def collect(x):
    n = lax.axis_size("seq")
    return lax.all_to_all(
        x.reshape(n, -1, x.shape[-1]), "seq", split_axis=0, concat_axis=0, tiled=True
    )


def head_slot():
    s, d = lax.axis_index("seq"), lax.axis_index("dp")
    n = lax.axis_size("seq")
    per = HEADS // lax.axis_size("dp")
    return (s + (n - per % n) * d) % n, per, n


def slot_place(d):
    s = lax.axis_index("seq")
    n = lax.axis_size("seq")
    per = HEADS // lax.axis_size("dp")
    j = (s + (n - per % n) * d) % n
    return jnp.where(j < per, (per * d + j - s) // n, HEADS // n)


def head_piece(x):
    if not ringed():
        return x
    rows = natural(gather_seq(x))
    rows = jnp.concatenate(rows + [jnp.zeros((HEAD, x.shape[1]), x.dtype)])
    return lax.dynamic_slice(rows, (head_slot()[0] * HEAD, 0), (HEAD, x.shape[1]))


def gather_head_rows(piece):
    n = lax.axis_size("seq")
    s = lax.axis_index("seq")
    rows, cols = piece.shape
    mine = HEADS // n
    if not ringed():
        full = lax.all_gather(piece, ("dp", "seq"), axis=0, tiled=True)
        picked = lax.dynamic_index_in_dim(full.reshape(mine, n, HEAD, cols), s, 1, keepdims=False)
        return picked.reshape(mine * HEAD, cols)
    owners = gather_z(pair_x(piece)).reshape(RING_Z * RING_X, HEAD, cols)
    per = head_slot()[1]
    return jnp.concatenate(
        [
            lax.dynamic_index_in_dim(owners, (n * p + s) // per, 0, keepdims=False)
            for p in range(mine)
        ]
    )


def split_head_rows(x):
    n = lax.axis_size("seq")
    s = lax.axis_index("seq")
    cols = x.shape[1]
    mine = HEADS // n
    if not ringed():
        full = jnp.zeros((mine, n, HEAD, cols), BF)
        full = lax.dynamic_update_index_in_dim(full, x.reshape(mine, 1, HEAD, cols), s, 1)
        return full.reshape(-1, cols), full.reshape(-1, cols)
    padded = jnp.concatenate([x, jnp.zeros((HEAD, cols), x.dtype)])
    slots = jnp.stack(
        [
            lax.dynamic_slice(padded, (slot_place(d) * HEAD, 0), (HEAD, cols))
            for d in range(lax.axis_size("dp"))
        ]
    )
    return split_x(slots)


def reduce_out_z(both):
    if not ringed():
        return lax.psum_scatter(both, ("dp", "seq"), scatter_dimension=0, tiled=True)
    return reduce_dp_z(both)


def head_rows_out(own):
    n = lax.axis_size("seq")
    s = lax.axis_index("seq")
    size = lax.axis_size("dp")
    cols = own.shape[-1]
    if not ringed():
        return own.astype(F32)
    pieces = gather_seq(own)
    per = HEADS // size
    d = lax.axis_index("dp")
    rows = jnp.concatenate(
        [
            lax.dynamic_index_in_dim(pieces, ((per * d + j) % n) ^ s, 0, keepdims=False)
            for j in range(per)
        ]
    )
    share = per * HEAD // n
    return lax.dynamic_slice(rows, (s * share, 0), (share, cols)).astype(F32)


def norm_forward(values, gain_vec):
    average = jnp.mean(values, axis=-1, keepdims=True)
    centred = values - average
    variance = jnp.mean(centred * centred, axis=-1, keepdims=True)
    inv_std = lax.rsqrt(variance + EPSILON)
    normal = centred * inv_std
    return normal, inv_std, (normal * gain_vec).astype(BF)


def norm_backward(grad_normed, normal, inv_std, gain_vec):
    grad_gain = jnp.sum(grad_normed * normal, axis=0)
    grad_hat = grad_normed * gain_vec
    mean_hat = jnp.mean(grad_hat, axis=-1, keepdims=True)
    mean_mix = jnp.mean(grad_hat * normal, axis=-1, keepdims=True)
    return inv_std * (grad_hat - mean_hat - normal * mean_mix), grad_gain


def flat(ref):
    value = ref[...]
    return value.reshape(value.shape[0] * value.shape[1] * value.shape[2], value.shape[3])


def turn(m, cos, up, down):
    return m * cos + pltpu.roll(m, PAIR - ROT // 2, 1) * up + pltpu.roll(m, ROT // 2, 1) * down


SCALE = 1.0 / math.sqrt(HEAD)


def soft(q, k, ok):
    scores = mm_t(q, k) * SCALE
    scores = jnp.where(ok > 0.0, scores, -1e30)
    top = jnp.max(scores, axis=-1, keepdims=True)
    e = jnp.exp(scores - top)
    return e * (1.0 / jnp.sum(e, axis=-1, keepdims=True))


def self_forward_kernel(ok_ref, cos_ref, up_ref, down_ref, q_ref, k_ref, v_ref, o_ref, qr_ref, kr_ref, vr_ref):
    cos, up, down = (r[...].reshape(-1, PAIR) for r in (cos_ref, up_ref, down_ref))
    q = turn(flat(q_ref), cos, up, down).astype(BF)
    k = turn(flat(k_ref), cos, up, down).astype(BF)
    v = flat(v_ref).astype(BF)
    ok = ok_ref[0]
    outs = []
    for h in (0, 1):
        sl = slice(h * HEAD, (h + 1) * HEAD)
        p = soft(q[:, sl], k[:, sl], ok).astype(BF)
        outs.append(mm(p, v[:, sl]))
    o_ref[...] = jnp.concatenate(outs, axis=1).astype(BF).reshape(o_ref.shape)
    qr_ref[...] = q.reshape(qr_ref.shape)
    kr_ref[...] = k.reshape(kr_ref.shape)
    vr_ref[...] = v.reshape(vr_ref.shape)


def pair_back(q, k, v, g, ok):
    dqs, dks, dvs = [], [], []
    for h in (0, 1):
        sl = slice(h * HEAD, (h + 1) * HEAD)
        p = soft(q[:, sl], k[:, sl], ok)
        dp = mm_t(g[:, sl], v[:, sl])
        inner = jnp.sum(p * dp, axis=-1, keepdims=True)
        ds = (p * (dp - inner)).astype(BF)
        dqs.append(mm(ds, k[:, sl]) * SCALE)
        dks.append(t_mm(ds, q[:, sl]) * SCALE)
        dvs.append(t_mm(p.astype(BF), g[:, sl]))
    return [jnp.concatenate(t, axis=1) for t in (dqs, dks, dvs)]


def self_backward_kernel(ok_ref, cos_ref, up_ref, down_ref, q_ref, k_ref, v_ref, g_ref, o_ref):
    cos, up, down = (r[...].reshape(-1, PAIR) for r in (cos_ref, up_ref, down_ref))
    dq, dk, dv = pair_back(flat(q_ref), flat(k_ref), flat(v_ref), flat(g_ref), ok_ref[0])
    dq = turn(dq, cos, -up, -down)
    dk = turn(dk, cos, -up, -down)
    pairs = o_ref.shape[3] // (3 * PAIR)
    hp = pl.program_id(1)
    shape = o_ref.shape[:3] + (PAIR,)
    for which, value in enumerate((dq, dk, dv)):
        at = pl.ds(pl.multiple_of((which * pairs + hp) * PAIR, PAIR), PAIR)
        o_ref[:, :, :, at] = value.astype(BF).reshape(shape)


def cross_forward_kernel(ok_ref, q_ref, k_ref, v_ref, o_ref):
    q, k, v = flat(q_ref), flat(k_ref), flat(v_ref)
    ok = ok_ref[0]
    outs = []
    for h in (0, 1):
        sl = slice(h * HEAD, (h + 1) * HEAD)
        p = soft(q[:, sl], k[:, sl], ok).astype(BF)
        outs.append(mm(p, v[:, sl]))
    o_ref[...] = jnp.concatenate(outs, axis=1).astype(BF).reshape(o_ref.shape)


def cross_backward_kernel(ok_ref, q_ref, k_ref, v_ref, g_ref, dq_ref, dkv_ref):
    dq, dk, dv = pair_back(flat(q_ref), flat(k_ref), flat(v_ref), flat(g_ref), ok_ref[0])
    dq_ref[...] = dq.astype(BF).reshape(dq_ref.shape)
    pairs = dkv_ref.shape[3] // (2 * PAIR)
    hp = pl.program_id(1)
    shape = dkv_ref.shape[:3] + (PAIR,)
    for which, value in enumerate((dk, dv)):
        at = pl.ds(pl.multiple_of((which * pairs + hp) * PAIR, PAIR), PAIR)
        dkv_ref[:, :, :, at] = value.astype(BF).reshape(shape)


def pair_spec(x, offset=0):
    r, _, t, _ = x.shape
    return pl.BlockSpec((r, 1, t, PAIR), lambda b, hp: (0, b, 0, offset + hp))


def wide_spec(r, t, width):
    return pl.BlockSpec((r, 1, t, width), lambda b, hp: (0, b, 0, 0))


def ok_spec(ok):
    return pl.BlockSpec((1, 1, ok.shape[2]), lambda b, hp: (b, 0, 0))


def table_spec(table):
    return pl.BlockSpec(table.shape, lambda b, hp: (0, 0, 0))


def cost(x, keys, products):
    r, b, t, width = x.shape
    return pl.CostEstimate(
        flops=2 * r * b * t * width * keys * products * 2,
        bytes_accessed=8 * x.size,
        transcendentals=r * b * t * keys * (width // HEAD),
    )


def self_forward(ok, tables, qk, v):
    r, b, t, width = v.shape
    pairs = width // PAIR
    shape = jax.ShapeDtypeStruct((r, b, t, pairs * PAIR), BF)
    return pl.pallas_call(
        self_forward_kernel,
        grid=(b, pairs),
        in_specs=[ok_spec(ok)]
        + [table_spec(x) for x in tables]
        + [pair_spec(qk), pair_spec(qk, pairs), pair_spec(v)],
        out_specs=[pair_spec(shape)] * 4,
        out_shape=[shape] * 4,
        cost_estimate=cost(shape, r * t, 2),
        name="self_forward",
    )(ok, *tables, qk, qk, v)


def self_backward(ok, tables, q, k, v, g):
    r, b, t, width = q.shape
    pairs = width // PAIR
    return pl.pallas_call(
        self_backward_kernel,
        grid=(b, pairs),
        in_specs=[ok_spec(ok)] + [table_spec(x) for x in tables] + [pair_spec(q)] * 4,
        out_specs=wide_spec(r, t, 3 * width),
        out_shape=jax.ShapeDtypeStruct((r, b, t, 3 * width), BF),
        cost_estimate=cost(q, r * t, 5),
        name="self_backward",
    )(ok, *tables, q, k, v, g)


def cross_forward(ok, q, kv):
    r, b, t, width = q.shape
    pairs = width // PAIR
    return pl.pallas_call(
        cross_forward_kernel,
        grid=(b, pairs),
        in_specs=[ok_spec(ok), pair_spec(q), pair_spec(kv), pair_spec(kv, pairs)],
        out_specs=pair_spec(q),
        out_shape=jax.ShapeDtypeStruct(q.shape, BF),
        cost_estimate=cost(q, r * kv.shape[2], 2),
        name="cross_forward",
    )(ok, q, kv, kv)


def cross_backward(ok, q, kv, g):
    r, b, t, width = q.shape
    pairs = width // PAIR
    return pl.pallas_call(
        cross_backward_kernel,
        grid=(b, pairs),
        in_specs=[ok_spec(ok), pair_spec(q), pair_spec(kv), pair_spec(kv, pairs), pair_spec(q)],
        out_specs=[pair_spec(q), wide_spec(r, kv.shape[2], kv.shape[3])],
        out_shape=[jax.ShapeDtypeStruct(q.shape, BF), jax.ShapeDtypeStruct(kv.shape, BF)],
        cost_estimate=cost(q, r * kv.shape[2], 5),
        name="cross_backward",
    )(ok, q, kv, kv, g)


def per_device(
    inputs,
    conditioning,
    seq_lengths,
    cond_lengths,
    gain_self,
    gain_cross,
    gain_mlp,
    w_query,
    w_key,
    w_value,
    w_output,
    c_query,
    c_key,
    c_value,
    c_output,
    w_gate,
    w_up,
    w_down,
    cotangent,
):
    batch, tokens_dev, width = inputs.shape
    cond_dev = conditioning.shape[1]
    n = lax.axis_size("seq")
    dp = lax.axis_size("dp")
    s = lax.axis_index("seq")
    d = lax.axis_index("dp")
    rel = jnp.arange(n) ^ s
    mine = width // n

    positions = rel[:, None] * tokens_dev + jnp.arange(tokens_dev)[None, :]
    key_ok = (positions.reshape(1, 1, -1) < seq_lengths[:, None, None]).astype(F32)
    cond_pos = rel[:, None] * cond_dev + jnp.arange(cond_dev)[None, :]
    cond_ok = (cond_pos.reshape(1, 1, -1) < cond_lengths[:, None, None]).astype(F32)
    half = ROT // 2
    inverse = 10000.0 ** (-jnp.arange(half).astype(F32) / half)
    angles = positions.astype(F32)[:, :, None] * inverse
    cosine, sine = jnp.cos(angles), jnp.sin(angles)
    one, nil = jnp.ones(cosine.shape[:2] + (HEAD - ROT,), F32), jnp.zeros_like(cosine)
    nil_rest = jnp.zeros_like(one)
    tables = [
        jnp.concatenate(parts + parts, axis=-1)
        for parts in (
            [cosine, cosine, one],
            [-sine, nil, nil_rest],
            [nil, sine, nil_rest],
        )
    ]

    gain_rows = jnp.stack([gain_self, gain_cross, gain_mlp]).astype(F32)
    share = gain_rows.shape[1]
    placed = lax.dynamic_update_slice(jnp.zeros((3, width), F32), gain_rows, (0, (d * n + s) * share))
    placed = placed + seq_swap(placed, 2)
    rows = batch * tokens_dev
    total = n * rows

    def cut(*mats):
        return jnp.concatenate([columns_out(w) for w in mats], axis=2)

    qk_part = deal(cut(w_query, w_key))
    qk_part, w_value, c_query, w_output, c_output = together(
        qk_part, w_value, c_query, w_output, c_output
    )

    qk_z = gather_dp_z(qk_part)
    vcq_z = gather_dp_z(deal(cut(w_value, c_query)))
    piece = head_piece(jnp.concatenate([w_output, c_output], axis=1))
    out_w = gather_head_rows(piece)
    qk_z, placed, tokens, given, c_key, c_value, w_gate, w_up, w_down = together(
        qk_z,
        placed,
        inputs.reshape(rows, width),
        conditioning.reshape(batch * cond_dev, width),
        c_key,
        c_value,
        w_gate,
        w_up,
        w_down,
    )
    qk_w = gather_dp_x(qk_z)
    gains = all_sum_dp(placed + seq_swap(placed, 1))
    tokens_all = gather_seq(tokens)
    gain_one, gain_two, gain_three = gains[0], gains[1], gains[2]
    ckv_z = gather_dp_z(deal(cut(c_key, c_value)))
    ffn_part = deal(hidden_out([w_gate, w_up, w_down]))
    cond_all = gather_seq(given).reshape(-1, width)
    hid = w_gate.shape[1] // wide()
    gather_ffn = gather_eight if ringed() else gather_seq
    shared = wide()

    normed_one = norm_forward(tokens_all.reshape(total, width).astype(F32), gain_one)[2]
    vcq_w = gather_dp_x(vcq_z)
    v_w, cq_w = vcq_w[:, :mine], vcq_w[:, mine:]
    qk = mm(normed_one, qk_w).reshape(n, batch, tokens_dev, 2 * mine)
    v_own = mm(normed_one, v_w).reshape(n, batch, tokens_dev, mine)
    qk, v_own, ffn_part = together(qk, v_own, ffn_part)
    attended, q_rot, k_rot, v_low = self_forward(key_ok, tables, qk, v_own)
    attended = attended.reshape(total, mine)
    ffn_w = deal_hidden_x(ffn_part)
    gu_w = gather_hidden(ffn_w[:, : 2 * hid])
    down_w = gather_hidden(ffn_w[:, 2 * hid :])
    attended, ffn_w, out_w = together(attended, ffn_w, out_w)
    w_out, c_out = out_w[:, :width], out_w[:, width:]
    partial = mm(attended, w_out).astype(BF).reshape(n, rows, width)
    partial, ckv_z = scatter_seq(partial, (ckv_z,))
    after_self = tokens.astype(F32) + partial
    normal_two, inv_two, own_two = norm_forward(after_self, gain_two)
    if ringed():
        normed_two, ckv_other = gather_seq(own_two, (x_swap(ckv_z),))
        ckv_w = gather_dp_x(ckv_z, ckv_other)
    else:
        normed_two, ckv_w = gather_seq(own_two), ckv_z
    normed_two = normed_two.reshape(total, width)
    cq = mm(normed_two, cq_w).astype(BF).reshape(n, batch, tokens_dev, mine)
    ckv = mm(cond_all, ckv_w).astype(BF).reshape(n, batch, cond_dev, 2 * mine)
    cq, incoming = together(cq, cotangent.reshape(rows, width))
    cross_att = cross_forward(cond_ok, cq, ckv).reshape(total, mine)
    if ringed():
        cross_att, *incoming_first = together(cross_att, *gather_eight_first(incoming))
    partial = mm(cross_att, c_out).astype(BF).reshape(n, rows, width)
    after_cross = after_self + scatter_seq(partial)
    after_cross, gu_w = together(after_cross, gu_w)
    normal_three, inv_three, own_three = norm_forward(after_cross, gain_three)
    normed_three = gather_ffn(own_three).reshape(shared * rows, width)
    if ringed():
        normed_three, *incoming_first = together(normed_three, *incoming_first)
        incoming_all = gather_eight_last(*incoming_first).reshape(shared * rows, width)
    else:
        incoming_all = gather_seq(incoming).reshape(total, width)
    gate = mm(normed_three, gu_w[:, :hid])
    gate, incoming_all = together(gate, incoming_all)
    up = mm(normed_three, gu_w[:, hid:])
    sig = jax.nn.sigmoid(gate)
    hidden = (gate * sig * up).astype(BF)
    grad_down = t_mm(incoming_all, hidden).astype(BF)
    incoming_all, grad_down = together(incoming_all, grad_down)
    d_hidden = mm(incoming_all, down_w)
    d_gate = (d_hidden * up * sig * (1.0 + gate * (1.0 - sig))).astype(BF)
    d_up = (d_hidden * gate * sig).astype(BF)
    d_gu = jnp.concatenate([d_gate, d_up], axis=1)
    own_down = reduce_hidden(grad_down)
    partial = mm_t(d_gu, gu_w).astype(BF).reshape(shared, rows, width)

    def block_product(now):
        _, late = together(now, hidden)
        return mm_t(late, down_w).astype(BF).reshape(shared, rows, width)

    def gu_product(now):
        _, late = together(now, d_gu)
        return t_mm(normed_three, late).astype(BF)

    if ringed():
        d_norm3, block_part, grad_gu = scatter_eight(partial, block_product, gu_product)
    else:
        d_norm3 = scatter_seq(partial)
        block_part, grad_gu = block_product(partial), gu_product(partial)
    d_norm3, own_down = together(d_norm3, own_down)
    own_gu = reduce_hidden(grad_gu)
    back, gain_grad_three = norm_backward(d_norm3, normal_three, inv_three, gain_three)
    d_after_cross = incoming.astype(F32) + back
    dc_low = gather_seq(d_after_cross.astype(BF)).reshape(total, width)
    d_catt = mm_t(dc_low, c_out).astype(BF).reshape(n, batch, tokens_dev, mine)
    grad_c_out = t_mm(cross_att, dc_low).astype(BF)
    d_cq, d_ckv = cross_backward(cond_ok, cq, ckv, d_catt)
    d_cq = d_cq.reshape(total, mine)
    d_ckv = d_ckv.reshape(n * batch * cond_dev, 2 * mine)
    partial = mm_t(d_cq, cq_w).astype(BF).reshape(n, rows, width)
    grad_cross = jnp.concatenate([t_mm(normed_two, d_cq), t_mm(cond_all, d_ckv)], axis=1).astype(BF)
    d_norm2, grad_cross = scatter_seq(partial, (grad_cross,))
    cross_both = reduce_hidden(grad_cross)
    partial = mm_t(d_ckv, ckv_w).astype(BF).reshape(n, batch * cond_dev, width)
    grad_cond = scatter_seq(partial)
    back, gain_grad_two = norm_backward(d_norm2, normal_two, inv_two, gain_two)
    d_after_self = d_after_cross + back
    if ringed():
        block_near, block_far = scatter_eight_x(block_part)
        ds_low, block_near, block_far = gather_seq(
            d_after_self.astype(BF), (block_near, block_far)
        )
    else:
        ds_low = gather_seq(d_after_self.astype(BF))
    ds_low = ds_low.reshape(total, width)
    ds_low, own_gu = together(ds_low, own_gu)
    ds_low, grad_c_out = together(ds_low, grad_c_out)
    d_att = mm_t(ds_low, w_out).astype(BF).reshape(n, batch, tokens_dev, mine)
    grad_out = t_mm(attended, ds_low).astype(BF)
    out_kept, out_away = split_head_rows(jnp.concatenate([grad_out, grad_c_out], axis=1))
    d_att, out_kept, out_away = together(d_att, out_kept, out_away)
    out_arrived = x_swap(out_away) if ringed() else out_away
    d_qkv = self_backward(key_ok, tables, q_rot, k_rot, v_low, d_att).reshape(total, 3 * mine)
    grad_qkv = t_mm(normed_one, d_qkv).astype(BF)
    d_qkv, grad_qkv = together(d_qkv, grad_qkv)
    qkv_kept, qkv_away = split_x(grad_qkv.reshape(dp, width // dp, grad_qkv.shape[1]))
    qkv_away, d_qkv = together(qkv_away, d_qkv)
    partial = mm_t(d_qkv, jnp.concatenate([qk_w, v_w], axis=1))
    partial = partial.astype(BF).reshape(n, rows, width)
    partial, out_arrived = together(partial, out_arrived)
    own_out = reduce_out_z(join_x(out_kept, out_arrived))
    qkv_arrived = dp_swap(qkv_away, 1) if ringed() else None
    if ringed():
        d_norm1, qkv_arrived, cross_both, own_out, block_arrived = scatter_seq(
            partial, (qkv_arrived, cross_both, own_out, seq_swap(block_far, 2))
        )
        block_sum = block_near + block_arrived.astype(F32)
    else:
        d_norm1 = scatter_seq(partial)
    qkv_both = join_x(qkv_kept, qkv_arrived)
    own_qkv = reduce_dp_z(qkv_both)
    own_ffn = jnp.concatenate([own_gu, own_down], axis=1)
    if ringed():
        qkv_both, own_ffn, cross_both = together(qkv_both, own_ffn, cross_both)
        ffn_kept, ffn_away = split_rows(own_ffn)
        own_ffn = join_hidden(ffn_kept, x_swap(ffn_away))
        cross_kept, cross_away = split_rows(cross_both)
        own_cross = join_x(cross_kept, x_swap(cross_away))
    else:
        block_sum, own_cross = scatter_seq(block_part), cross_both
    block = (after_cross + block_sum).astype(BF)
    own_ffn = collect(own_ffn)
    own_ffn, own_qkv = together(own_ffn, own_qkv)
    normal_one, inv_one, _ = norm_forward(tokens.astype(F32), gain_one)
    back, gain_grad_one = norm_backward(d_norm1, normal_one, inv_one, gain_one)
    grad_in = d_after_self + back

    own_gate, own_up, own_down = part_hidden(own_ffn, 3)
    own_cross = collect(own_cross)
    own_out = head_rows_out(own_out)
    own_qkv = collect(own_qkv)
    g_q, g_k, g_v = (columns_back(own_qkv[:, :, i * mine : (i + 1) * mine]) for i in range(3))
    g_cq, g_ck, g_cv = (columns_back(own_cross[:, :, i * mine : (i + 1) * mine]) for i in range(3))
    gain_grads = all_sum(jnp.stack([gain_grad_one, gain_grad_two, gain_grad_three]))
    gain_grads = lax.dynamic_slice(gain_grads, (0, (d * n + s) * share), (3, share))

    def f32(x):
        return x.astype(F32)

    return (
        block.reshape(inputs.shape),
        grad_in.reshape(inputs.shape),
        grad_cond.reshape(conditioning.shape),
        gain_grads[0],
        gain_grads[1],
        gain_grads[2],
        f32(g_q),
        f32(g_k),
        f32(g_v),
        f32(own_out[:, :width]),
        f32(g_cq),
        f32(g_ck),
        f32(g_cv),
        f32(own_out[:, width:]),
        f32(own_gate),
        f32(own_up),
        f32(own_down),
    )


def solution(mesh):
    rows = P("dp", "seq", None)
    split = P(("dp", "seq"))
    matrix = P(("dp", "seq"), None)
    return jax.shard_map(
        per_device,
        mesh=mesh,
        in_specs=(rows, rows, P("dp"), P("dp"), split, split, split) + (matrix,) * 11 + (rows,),
        out_specs=(rows, rows, rows, split, split, split) + (matrix,) * 11,
        check_vma=False,
    )
```

```python
import functools
import math

import jax
import jax.numpy as jnp
from jax import lax
from jax.experimental import pallas as pl
from jax.experimental.pallas import tpu as pltpu
from jax.sharding import PartitionSpec as P

HEADS = 24
HEAD = 64
ROT = 32
EPSILON = 1e-05
BF = jnp.bfloat16
F32 = jnp.float32
PAIR = 2 * HEAD


def mm(left, right):
    return jnp.dot(left, right, preferred_element_type=F32)


def mm_t(left, right):
    return lax.dot_general(left, right, (((1,), (1,)), ((), ())), preferred_element_type=F32)


def t_mm(left, right):
    return lax.dot_general(left, right, (((0,), (0,)), ((), ())), preferred_element_type=F32)


def seq_swap(x, mask):
    n = lax.axis_size("seq")
    return lax.ppermute(x, "seq", [(i, i ^ mask) for i in range(n)])


def dp_swap(x, mask):
    n = lax.axis_size("dp")
    return lax.ppermute(x, "dp", [(i, i ^ mask) for i in range(n)])


def all_sum_dp(v):
    mask = lax.axis_size("dp") // 2
    while mask:
        v = v + dp_swap(v, mask)
        mask //= 2
    return v


def gather_seq(x, beside=()):
    core = seq_swap(x, 1)
    far = seq_swap(x, 2)
    if beside:
        far, *beside = together(far, *beside)
    diag = seq_swap(far, 1)
    blocks = jnp.stack([x, core, far, diag])
    return (blocks, *beside) if beside else blocks


def scatter_seq(partial, beside=()):
    far = partial[2].astype(F32) + seq_swap(partial[3], 1).astype(F32)
    arrived = seq_swap(far.astype(BF), 2)
    arrived, *beside = together(arrived, *beside)
    near = partial[0].astype(F32) + seq_swap(partial[1], 1).astype(F32)
    total = near + arrived.astype(F32)
    return (total, *beside) if beside else total


def x_swap(x):
    return dp_swap(x, 1)


def all_sum(v):
    for mask in (2, 1):
        v = v + seq_swap(v, mask)
    return all_sum_dp(v)


def natural(blocks):
    s = lax.axis_index("seq")
    n = lax.axis_size("seq")
    return [lax.dynamic_index_in_dim(blocks, k ^ s, 0, keepdims=False) for k in range(n)]


def gather_eight_first(x):
    return x, seq_swap(x, 2), x_swap(x)


def gather_eight(x):
    return gather_eight_last(*gather_eight_first(x))


def gather_eight_last(x, far, side):
    half = x.shape[0] // 2
    corner = jnp.concatenate([x_swap(far[:half]), seq_swap(side[half:], 2)])
    blocks = []
    for near in (x, far, side, corner):
        blocks += [near, seq_swap(near, 1)]
    return jnp.stack(blocks)


def scatter_eight(partial, first=None, second=None):
    half = partial.shape[1] // 2

    def with_core(k):
        return partial[k].astype(F32) + seq_swap(partial[k + 1], 1).astype(F32)

    corner = with_core(6).astype(BF)
    corner, partial = together(corner, partial)
    from_x, from_y = x_swap(corner[:half]), seq_swap(corner[half:], 2)
    out = []
    if first is not None:
        value = first(corner)
        from_x, from_y, value = together(from_x, from_y, value)
        out.append(value)
    far = with_core(2)
    far = jnp.concatenate([far[:half] + from_x.astype(F32), far[half:]]).astype(BF)
    side = with_core(4)
    side = jnp.concatenate([side[:half], side[half:] + from_y.astype(F32)]).astype(BF)
    far, side = together(far, side)
    from_y, from_x = seq_swap(far, 2), x_swap(side)
    if second is not None:
        value = second(far)
        from_y, from_x, value = together(from_y, from_x, value)
        out.append(value)
    return (with_core(0) + from_y.astype(F32) + from_x.astype(F32), *out)


def scatter_eight_x(partial):
    def with_core(k):
        return partial[k].astype(F32) + seq_swap(partial[k + 1], 1).astype(F32)

    away = jnp.stack([with_core(4).astype(BF), with_core(6).astype(BF)])
    arrived = x_swap(away)
    near = with_core(0) + arrived[0].astype(F32)
    return near, (with_core(2) + arrived[1].astype(F32)).astype(BF)


def together(*values):
    return lax.optimization_barrier(values)


RING_Z, RING_X = 4, 2


def ringed():
    return lax.axis_size("dp") == RING_Z * RING_X


def z_groups():
    return [[z * RING_X + x for z in range(RING_Z)] for x in range(RING_X)]


def gather_z(chunk):
    return lax.all_gather(chunk, "dp", axis=0, axis_index_groups=z_groups())


def gather_dp_z(chunk):
    if not ringed():
        return lax.all_gather(chunk, "dp", axis=0, tiled=True)
    return gather_z(chunk)


def pair_x(chunk):
    if not ringed():
        return chunk
    other = x_swap(chunk)
    first = lax.axis_index("dp") % RING_X == 0
    return jnp.concatenate([jnp.where(first, chunk, other), jnp.where(first, other, chunk)])


def gather_dp_x(own, other=None):
    if not ringed():
        return own
    cols = own.shape[2]
    first = lax.axis_index("dp") % RING_X == 0
    other = dp_swap(own, 1) if other is None else other
    both = jnp.stack([jnp.where(first, own, other), jnp.where(first, other, own)], axis=1)
    return both.reshape(-1, cols)


def reduce_dp_x(slots):
    kept, away = split_x(slots)
    return join_x(kept, x_swap(away) if ringed() else None)


def split_x(slots):
    n, rows, cols = slots.shape
    if not ringed():
        return slots, slots
    xx = lax.axis_index("dp") % RING_X
    split = slots.reshape(RING_Z, RING_X, rows, cols)
    away = lax.dynamic_index_in_dim(split, 1 - xx, axis=1, keepdims=False)
    kept = lax.dynamic_index_in_dim(split, xx, axis=1, keepdims=False)
    return kept, away


def join_x(kept, arrived):
    if ringed():
        kept = (kept.astype(F32) + arrived.astype(F32)).astype(BF)
    return kept.reshape(-1, kept.shape[-1])


def reduce_dp_z(both):
    if not ringed():
        return lax.psum_scatter(both, "dp", scatter_dimension=0, tiled=True)
    return lax.psum_scatter(
        both, "dp", scatter_dimension=0, tiled=True, axis_index_groups=z_groups()
    )


def reduce_dp(slots):
    return reduce_dp_z(reduce_dp_x(slots))


def wide():
    return lax.axis_size("seq") * (RING_X if ringed() else 1)


def hidden_out(mats):
    n = lax.axis_size("seq")
    parts = wide() // n
    rows = mats[0].shape[0]
    cut = [m.reshape(rows, n, parts, -1) for m in mats]
    return jnp.concatenate(cut, axis=3).transpose(1, 0, 2, 3).reshape(n, rows, -1)


def deal_hidden_x(got):
    if not ringed():
        return got
    rows = got.shape[0]
    xx = lax.axis_index("dp") % RING_X
    cut = got.reshape(rows, RING_X, -1)
    kept = lax.dynamic_index_in_dim(cut, xx, 1, keepdims=False)
    arrived = x_swap(lax.dynamic_index_in_dim(cut, 1 - xx, 1, keepdims=False))
    first = xx == 0
    return jnp.concatenate([jnp.where(first, kept, arrived), jnp.where(first, arrived, kept)])


def gather_hidden(x):
    if not ringed():
        return lax.all_gather(x, "dp", axis=0, tiled=True)
    return lax.all_gather(x, "dp", axis=0, tiled=True, axis_index_groups=z_groups())


def reduce_hidden(grad):
    if not ringed():
        return lax.psum_scatter(grad, "dp", scatter_dimension=0, tiled=True)
    return lax.psum_scatter(
        grad, "dp", scatter_dimension=0, tiled=True, axis_index_groups=z_groups()
    )


def split_rows(x):
    xx = lax.axis_index("dp") % RING_X
    cut = x.reshape(RING_X, -1, x.shape[1])
    kept = lax.dynamic_index_in_dim(cut, xx, 0, keepdims=False)
    return kept, lax.dynamic_index_in_dim(cut, 1 - xx, 0, keepdims=False)


def join_hidden(kept, arrived):
    first = lax.axis_index("dp") % RING_X == 0
    return jnp.concatenate(
        [jnp.where(first, kept, arrived), jnp.where(first, arrived, kept)], axis=1
    )


def part_hidden(got, count):
    n = lax.axis_size("seq")
    parts = wide() // n
    rows = got.shape[1]
    got = got.reshape(n, rows, parts, count, -1)
    return [got[:, :, :, i].transpose(1, 0, 2, 3).reshape(rows, -1) for i in range(count)]


def columns_out(x):
    rows = x.shape[0]
    n = lax.axis_size("seq")
    return x.reshape(rows, HEADS // n, n, HEAD).transpose(2, 0, 1, 3).reshape(n, rows, -1)


def columns_back(x):
    n, rows, _ = x.shape
    return x.reshape(n, rows, HEADS // n, HEAD).transpose(1, 2, 0, 3).reshape(rows, HEADS * HEAD)


def deal(x):
    got = lax.all_to_all(x, "seq", split_axis=0, concat_axis=0, tiled=True)
    return got.reshape(-1, x.shape[-1])


def collect(x):
    n = lax.axis_size("seq")
    return lax.all_to_all(
        x.reshape(n, -1, x.shape[-1]), "seq", split_axis=0, concat_axis=0, tiled=True
    )


def head_slot():
    s, d = lax.axis_index("seq"), lax.axis_index("dp")
    n = lax.axis_size("seq")
    per = HEADS // lax.axis_size("dp")
    return (s + (n - per % n) * d) % n, per, n


def slot_place(d):
    s = lax.axis_index("seq")
    n = lax.axis_size("seq")
    per = HEADS // lax.axis_size("dp")
    j = (s + (n - per % n) * d) % n
    return jnp.where(j < per, (per * d + j - s) // n, HEADS // n)


def head_piece(x):
    if not ringed():
        return x
    rows = natural(gather_seq(x))
    rows = jnp.concatenate(rows + [jnp.zeros((HEAD, x.shape[1]), x.dtype)])
    return lax.dynamic_slice(rows, (head_slot()[0] * HEAD, 0), (HEAD, x.shape[1]))


def gather_head_rows(piece):
    n = lax.axis_size("seq")
    s = lax.axis_index("seq")
    rows, cols = piece.shape
    mine = HEADS // n
    if not ringed():
        full = lax.all_gather(piece, ("dp", "seq"), axis=0, tiled=True)
        picked = lax.dynamic_index_in_dim(full.reshape(mine, n, HEAD, cols), s, 1, keepdims=False)
        return picked.reshape(mine * HEAD, cols)
    owners = gather_z(pair_x(piece)).reshape(RING_Z * RING_X, HEAD, cols)
    per = head_slot()[1]
    return jnp.concatenate(
        [
            lax.dynamic_index_in_dim(owners, (n * p + s) // per, 0, keepdims=False)
            for p in range(mine)
        ]
    )


def split_head_rows(x):
    n = lax.axis_size("seq")
    s = lax.axis_index("seq")
    cols = x.shape[1]
    mine = HEADS // n
    if not ringed():
        full = jnp.zeros((mine, n, HEAD, cols), BF)
        full = lax.dynamic_update_index_in_dim(full, x.reshape(mine, 1, HEAD, cols), s, 1)
        return full.reshape(-1, cols), full.reshape(-1, cols)
    padded = jnp.concatenate([x, jnp.zeros((HEAD, cols), x.dtype)])
    slots = jnp.stack(
        [
            lax.dynamic_slice(padded, (slot_place(d) * HEAD, 0), (HEAD, cols))
            for d in range(lax.axis_size("dp"))
        ]
    )
    return split_x(slots)


def reduce_out_z(both):
    if not ringed():
        return lax.psum_scatter(both, ("dp", "seq"), scatter_dimension=0, tiled=True)
    return reduce_dp_z(both)


def head_rows_out(own):
    n = lax.axis_size("seq")
    s = lax.axis_index("seq")
    size = lax.axis_size("dp")
    cols = own.shape[-1]
    if not ringed():
        return own.astype(F32)
    pieces = gather_seq(own)
    per = HEADS // size
    d = lax.axis_index("dp")
    rows = jnp.concatenate(
        [
            lax.dynamic_index_in_dim(pieces, ((per * d + j) % n) ^ s, 0, keepdims=False)
            for j in range(per)
        ]
    )
    share = per * HEAD // n
    return lax.dynamic_slice(rows, (s * share, 0), (share, cols)).astype(F32)


def norm_forward(values, gain_vec):
    average = jnp.mean(values, axis=-1, keepdims=True)
    centred = values - average
    variance = jnp.mean(centred * centred, axis=-1, keepdims=True)
    inv_std = lax.rsqrt(variance + EPSILON)
    normal = centred * inv_std
    return normal, inv_std, (normal * gain_vec).astype(BF)


def norm_backward(grad_normed, normal, inv_std, gain_vec):
    grad_gain = jnp.sum(grad_normed * normal, axis=0)
    grad_hat = grad_normed * gain_vec
    mean_hat = jnp.mean(grad_hat, axis=-1, keepdims=True)
    mean_mix = jnp.mean(grad_hat * normal, axis=-1, keepdims=True)
    return inv_std * (grad_hat - mean_hat - normal * mean_mix), grad_gain


def flat(ref):
    value = ref[...]
    return value.reshape(value.shape[0] * value.shape[1] * value.shape[2], value.shape[3])


def turn(m, cos, up, down):
    return m * cos + pltpu.roll(m, PAIR - ROT // 2, 1) * up + pltpu.roll(m, ROT // 2, 1) * down


SCALE = 1.0 / math.sqrt(HEAD)


def soft(q, k, ok):
    scores = mm_t(q, k) * SCALE
    scores = jnp.where(ok > 0.0, scores, -1e30)
    top = jnp.max(scores, axis=-1, keepdims=True)
    e = jnp.exp(scores - top)
    return e * (1.0 / jnp.sum(e, axis=-1, keepdims=True))


def self_forward_kernel(ok_ref, cos_ref, up_ref, down_ref, q_ref, k_ref, v_ref, o_ref, qr_ref, kr_ref, vr_ref):
    cos, up, down = (r[...].reshape(-1, PAIR) for r in (cos_ref, up_ref, down_ref))
    q = turn(flat(q_ref), cos, up, down).astype(BF)
    k = turn(flat(k_ref), cos, up, down).astype(BF)
    v = flat(v_ref).astype(BF)
    ok = ok_ref[0]
    outs = []
    for h in (0, 1):
        sl = slice(h * HEAD, (h + 1) * HEAD)
        p = soft(q[:, sl], k[:, sl], ok).astype(BF)
        outs.append(mm(p, v[:, sl]))
    o_ref[...] = jnp.concatenate(outs, axis=1).astype(BF).reshape(o_ref.shape)
    qr_ref[...] = q.reshape(qr_ref.shape)
    kr_ref[...] = k.reshape(kr_ref.shape)
    vr_ref[...] = v.reshape(vr_ref.shape)


def pair_back(q, k, v, g, ok):
    dqs, dks, dvs = [], [], []
    for h in (0, 1):
        sl = slice(h * HEAD, (h + 1) * HEAD)
        p = soft(q[:, sl], k[:, sl], ok)
        dp = mm_t(g[:, sl], v[:, sl])
        inner = jnp.sum(p * dp, axis=-1, keepdims=True)
        ds = (p * (dp - inner)).astype(BF)
        dqs.append(mm(ds, k[:, sl]) * SCALE)
        dks.append(t_mm(ds, q[:, sl]) * SCALE)
        dvs.append(t_mm(p.astype(BF), g[:, sl]))
    return [jnp.concatenate(t, axis=1) for t in (dqs, dks, dvs)]


def self_backward_kernel(ok_ref, cos_ref, up_ref, down_ref, q_ref, k_ref, v_ref, g_ref, o_ref):
    cos, up, down = (r[...].reshape(-1, PAIR) for r in (cos_ref, up_ref, down_ref))
    dq, dk, dv = pair_back(flat(q_ref), flat(k_ref), flat(v_ref), flat(g_ref), ok_ref[0])
    dq = turn(dq, cos, -up, -down)
    dk = turn(dk, cos, -up, -down)
    pairs = o_ref.shape[3] // (3 * PAIR)
    hp = pl.program_id(1)
    shape = o_ref.shape[:3] + (PAIR,)
    for which, value in enumerate((dq, dk, dv)):
        at = pl.ds(pl.multiple_of((which * pairs + hp) * PAIR, PAIR), PAIR)
        o_ref[:, :, :, at] = value.astype(BF).reshape(shape)


def cross_forward_kernel(ok_ref, q_ref, k_ref, v_ref, o_ref):
    q, k, v = flat(q_ref), flat(k_ref), flat(v_ref)
    ok = ok_ref[0]
    outs = []
    for h in (0, 1):
        sl = slice(h * HEAD, (h + 1) * HEAD)
        p = soft(q[:, sl], k[:, sl], ok).astype(BF)
        outs.append(mm(p, v[:, sl]))
    o_ref[...] = jnp.concatenate(outs, axis=1).astype(BF).reshape(o_ref.shape)


def cross_backward_kernel(ok_ref, q_ref, k_ref, v_ref, g_ref, dq_ref, dkv_ref):
    dq, dk, dv = pair_back(flat(q_ref), flat(k_ref), flat(v_ref), flat(g_ref), ok_ref[0])
    dq_ref[...] = dq.astype(BF).reshape(dq_ref.shape)
    pairs = dkv_ref.shape[3] // (2 * PAIR)
    hp = pl.program_id(1)
    shape = dkv_ref.shape[:3] + (PAIR,)
    for which, value in enumerate((dk, dv)):
        at = pl.ds(pl.multiple_of((which * pairs + hp) * PAIR, PAIR), PAIR)
        dkv_ref[:, :, :, at] = value.astype(BF).reshape(shape)


def pair_spec(x, offset=0):
    r, _, t, _ = x.shape
    return pl.BlockSpec((r, 1, t, PAIR), lambda b, hp: (0, b, 0, offset + hp))


def wide_spec(r, t, width):
    return pl.BlockSpec((r, 1, t, width), lambda b, hp: (0, b, 0, 0))


def ok_spec(ok):
    return pl.BlockSpec((1, 1, ok.shape[2]), lambda b, hp: (b, 0, 0))


def table_spec(table):
    return pl.BlockSpec(table.shape, lambda b, hp: (0, 0, 0))


def cost(x, keys, products):
    r, b, t, width = x.shape
    return pl.CostEstimate(
        flops=2 * r * b * t * width * keys * products * 2,
        bytes_accessed=8 * x.size,
        transcendentals=r * b * t * keys * (width // HEAD),
    )


def self_forward(ok, tables, qk, v):
    r, b, t, width = v.shape
    pairs = width // PAIR
    shape = jax.ShapeDtypeStruct((r, b, t, pairs * PAIR), BF)
    return pl.pallas_call(
        self_forward_kernel,
        grid=(b, pairs),
        in_specs=[ok_spec(ok)]
        + [table_spec(x) for x in tables]
        + [pair_spec(qk), pair_spec(qk, pairs), pair_spec(v)],
        out_specs=[pair_spec(shape)] * 4,
        out_shape=[shape] * 4,
        cost_estimate=cost(shape, r * t, 2),
        name="self_forward",
    )(ok, *tables, qk, qk, v)


def self_backward(ok, tables, q, k, v, g):
    r, b, t, width = q.shape
    pairs = width // PAIR
    return pl.pallas_call(
        self_backward_kernel,
        grid=(b, pairs),
        in_specs=[ok_spec(ok)] + [table_spec(x) for x in tables] + [pair_spec(q)] * 4,
        out_specs=wide_spec(r, t, 3 * width),
        out_shape=jax.ShapeDtypeStruct((r, b, t, 3 * width), BF),
        cost_estimate=cost(q, r * t, 5),
        name="self_backward",
    )(ok, *tables, q, k, v, g)


def cross_forward(ok, q, kv):
    r, b, t, width = q.shape
    pairs = width // PAIR
    return pl.pallas_call(
        cross_forward_kernel,
        grid=(b, pairs),
        in_specs=[ok_spec(ok), pair_spec(q), pair_spec(kv), pair_spec(kv, pairs)],
        out_specs=pair_spec(q),
        out_shape=jax.ShapeDtypeStruct(q.shape, BF),
        cost_estimate=cost(q, r * kv.shape[2], 2),
        name="cross_forward",
    )(ok, q, kv, kv)


def cross_backward(ok, q, kv, g):
    r, b, t, width = q.shape
    pairs = width // PAIR
    return pl.pallas_call(
        cross_backward_kernel,
        grid=(b, pairs),
        in_specs=[ok_spec(ok), pair_spec(q), pair_spec(kv), pair_spec(kv, pairs), pair_spec(q)],
        out_specs=[pair_spec(q), wide_spec(r, kv.shape[2], kv.shape[3])],
        out_shape=[jax.ShapeDtypeStruct(q.shape, BF), jax.ShapeDtypeStruct(kv.shape, BF)],
        cost_estimate=cost(q, r * kv.shape[2], 5),
        name="cross_backward",
    )(ok, q, kv, kv, g)


def per_device(
    inputs,
    conditioning,
    seq_lengths,
    cond_lengths,
    gain_self,
    gain_cross,
    gain_mlp,
    w_query,
    w_key,
    w_value,
    w_output,
    c_query,
    c_key,
    c_value,
    c_output,
    w_gate,
    w_up,
    w_down,
    cotangent,
):
    batch, tokens_dev, width = inputs.shape
    cond_dev = conditioning.shape[1]
    n = lax.axis_size("seq")
    dp = lax.axis_size("dp")
    s = lax.axis_index("seq")
    d = lax.axis_index("dp")
    rel = jnp.arange(n) ^ s
    mine = width // n

    positions = rel[:, None] * tokens_dev + jnp.arange(tokens_dev)[None, :]
    key_ok = (positions.reshape(1, 1, -1) < seq_lengths[:, None, None]).astype(F32)
    cond_pos = rel[:, None] * cond_dev + jnp.arange(cond_dev)[None, :]
    cond_ok = (cond_pos.reshape(1, 1, -1) < cond_lengths[:, None, None]).astype(F32)
    half = ROT // 2
    inverse = 10000.0 ** (-jnp.arange(half).astype(F32) / half)
    angles = positions.astype(F32)[:, :, None] * inverse
    cosine, sine = jnp.cos(angles), jnp.sin(angles)
    one, nil = jnp.ones(cosine.shape[:2] + (HEAD - ROT,), F32), jnp.zeros_like(cosine)
    nil_rest = jnp.zeros_like(one)
    tables = [
        jnp.concatenate(parts + parts, axis=-1)
        for parts in (
            [cosine, cosine, one],
            [-sine, nil, nil_rest],
            [nil, sine, nil_rest],
        )
    ]

    gain_rows = jnp.stack([gain_self, gain_cross, gain_mlp]).astype(F32)
    share = gain_rows.shape[1]
    placed = lax.dynamic_update_slice(jnp.zeros((3, width), F32), gain_rows, (0, (d * n + s) * share))
    placed = placed + seq_swap(placed, 2)
    rows = batch * tokens_dev
    total = n * rows

    def cut(*mats):
        return jnp.concatenate([columns_out(w) for w in mats], axis=2)

    qk_part = deal(cut(w_query, w_key))
    qk_part, w_value, c_query, w_output, c_output = together(
        qk_part, w_value, c_query, w_output, c_output
    )

    qk_z = gather_dp_z(qk_part)
    vcq_z = gather_dp_z(deal(cut(w_value, c_query)))
    piece = head_piece(jnp.concatenate([w_output, c_output], axis=1))
    out_w = gather_head_rows(piece)
    qk_z, placed, tokens, given, c_key, c_value, w_gate, w_up, w_down = together(
        qk_z,
        placed,
        inputs.reshape(rows, width),
        conditioning.reshape(batch * cond_dev, width),
        c_key,
        c_value,
        w_gate,
        w_up,
        w_down,
    )
    qk_w = gather_dp_x(qk_z)
    gains = all_sum_dp(placed + seq_swap(placed, 1))
    tokens_all = gather_seq(tokens)
    gain_one, gain_two, gain_three = gains[0], gains[1], gains[2]
    ckv_z = gather_dp_z(deal(cut(c_key, c_value)))
    ffn_part = deal(hidden_out([w_gate, w_up, w_down]))
    cond_all = gather_seq(given).reshape(-1, width)
    hid = w_gate.shape[1] // wide()
    gather_ffn = gather_eight if ringed() else gather_seq
    shared = wide()

    normed_one = norm_forward(tokens_all.reshape(total, width).astype(F32), gain_one)[2]
    vcq_w = gather_dp_x(vcq_z)
    v_w, cq_w = vcq_w[:, :mine], vcq_w[:, mine:]
    qk = mm(normed_one, qk_w).reshape(n, batch, tokens_dev, 2 * mine)
    v_own = mm(normed_one, v_w).reshape(n, batch, tokens_dev, mine)
    qk, v_own, ffn_part = together(qk, v_own, ffn_part)
    attended, q_rot, k_rot, v_low = self_forward(key_ok, tables, qk, v_own)
    attended = attended.reshape(total, mine)
    ffn_w = deal_hidden_x(ffn_part)
    gu_w = gather_hidden(ffn_w[:, : 2 * hid])
    down_w = gather_hidden(ffn_w[:, 2 * hid :])
    attended, ffn_w, out_w = together(attended, ffn_w, out_w)
    w_out, c_out = out_w[:, :width], out_w[:, width:]
    partial = mm(attended, w_out).astype(BF).reshape(n, rows, width)
    partial, ckv_z = scatter_seq(partial, (ckv_z,))
    after_self = tokens.astype(F32) + partial
    normal_two, inv_two, own_two = norm_forward(after_self, gain_two)
    if ringed():
        normed_two, ckv_other = gather_seq(own_two, (x_swap(ckv_z),))
        ckv_w = gather_dp_x(ckv_z, ckv_other)
    else:
        normed_two, ckv_w = gather_seq(own_two), ckv_z
    normed_two = normed_two.reshape(total, width)
    cq = mm(normed_two, cq_w).astype(BF).reshape(n, batch, tokens_dev, mine)
    ckv = mm(cond_all, ckv_w).astype(BF).reshape(n, batch, cond_dev, 2 * mine)
    cq, incoming = together(cq, cotangent.reshape(rows, width))
    cross_att = cross_forward(cond_ok, cq, ckv).reshape(total, mine)
    if ringed():
        cross_att, *incoming_first = together(cross_att, *gather_eight_first(incoming))
    partial = mm(cross_att, c_out).astype(BF).reshape(n, rows, width)
    after_cross = after_self + scatter_seq(partial)
    after_cross, gu_w = together(after_cross, gu_w)
    normal_three, inv_three, own_three = norm_forward(after_cross, gain_three)
    normed_three = gather_ffn(own_three).reshape(shared * rows, width)
    if ringed():
        normed_three, *incoming_first = together(normed_three, *incoming_first)
        incoming_all = gather_eight_last(*incoming_first).reshape(shared * rows, width)
    else:
        incoming_all = gather_seq(incoming).reshape(total, width)
    gate = mm(normed_three, gu_w[:, :hid])
    gate, incoming_all = together(gate, incoming_all)
    up = mm(normed_three, gu_w[:, hid:])
    sig = jax.nn.sigmoid(gate)
    hidden = (gate * sig * up).astype(BF)
    grad_down = t_mm(incoming_all, hidden).astype(BF)
    incoming_all, grad_down = together(incoming_all, grad_down)
    d_hidden = mm(incoming_all, down_w)
    d_gate = (d_hidden * up * sig * (1.0 + gate * (1.0 - sig))).astype(BF)
    d_up = (d_hidden * gate * sig).astype(BF)
    d_gu = jnp.concatenate([d_gate, d_up], axis=1)
    own_down = reduce_hidden(grad_down)
    partial = mm_t(d_gu, gu_w).astype(BF).reshape(shared, rows, width)

    def block_product(now):
        _, late = together(now, hidden)
        return mm_t(late, down_w).astype(BF).reshape(shared, rows, width)

    def gu_product(now):
        _, late = together(now, d_gu)
        return t_mm(normed_three, late).astype(BF)

    if ringed():
        d_norm3, block_part, grad_gu = scatter_eight(partial, block_product, gu_product)
    else:
        d_norm3 = scatter_seq(partial)
        block_part, grad_gu = block_product(partial), gu_product(partial)
    d_norm3, own_down = together(d_norm3, own_down)
    own_gu = reduce_hidden(grad_gu)
    back, gain_grad_three = norm_backward(d_norm3, normal_three, inv_three, gain_three)
    d_after_cross = incoming.astype(F32) + back
    dc_low = gather_seq(d_after_cross.astype(BF)).reshape(total, width)
    d_catt = mm_t(dc_low, c_out).astype(BF).reshape(n, batch, tokens_dev, mine)
    grad_c_out = t_mm(cross_att, dc_low).astype(BF)
    d_cq, d_ckv = cross_backward(cond_ok, cq, ckv, d_catt)
    d_cq = d_cq.reshape(total, mine)
    d_ckv = d_ckv.reshape(n * batch * cond_dev, 2 * mine)
    partial = mm_t(d_cq, cq_w).astype(BF).reshape(n, rows, width)
    grad_cross = jnp.concatenate([t_mm(normed_two, d_cq), t_mm(cond_all, d_ckv)], axis=1).astype(BF)
    d_norm2, grad_cross = scatter_seq(partial, (grad_cross,))
    cross_both = reduce_hidden(grad_cross)
    partial = mm_t(d_ckv, ckv_w).astype(BF).reshape(n, batch * cond_dev, width)
    grad_cond = scatter_seq(partial)
    back, gain_grad_two = norm_backward(d_norm2, normal_two, inv_two, gain_two)
    d_after_self = d_after_cross + back
    if ringed():
        block_near, block_far = scatter_eight_x(block_part)
        ds_low, block_near, block_far = gather_seq(
            d_after_self.astype(BF), (block_near, block_far)
        )
    else:
        ds_low = gather_seq(d_after_self.astype(BF))
    ds_low = ds_low.reshape(total, width)
    ds_low, own_gu, own_down = together(ds_low, own_gu, own_down)
    own_ffn = jnp.concatenate([own_gu, own_down], axis=1)
    if ringed():
        ffn_kept, ffn_away = split_rows(own_ffn)
        ffn_arrived = x_swap(ffn_away)
    ds_low, grad_c_out = together(ds_low, grad_c_out)
    d_att = mm_t(ds_low, w_out).astype(BF).reshape(n, batch, tokens_dev, mine)
    grad_out = t_mm(attended, ds_low).astype(BF)
    out_kept, out_away = split_head_rows(jnp.concatenate([grad_out, grad_c_out], axis=1))
    d_att, out_kept, out_away = together(d_att, out_kept, out_away)
    out_arrived = x_swap(out_away) if ringed() else out_away
    d_qkv = self_backward(key_ok, tables, q_rot, k_rot, v_low, d_att).reshape(total, 3 * mine)
    if ringed():
        d_qkv, ffn_arrived = together(d_qkv, ffn_arrived)
        own_ffn = join_hidden(ffn_kept, ffn_arrived)
    own_ffn = collect(own_ffn)
    grad_qkv = t_mm(normed_one, d_qkv).astype(BF)
    d_qkv, grad_qkv = together(d_qkv, grad_qkv)
    qkv_kept, qkv_away = split_x(grad_qkv.reshape(dp, width // dp, grad_qkv.shape[1]))
    qkv_away, d_qkv = together(qkv_away, d_qkv)
    partial = mm_t(d_qkv, jnp.concatenate([qk_w, v_w], axis=1))
    partial = partial.astype(BF).reshape(n, rows, width)
    partial, out_arrived = together(partial, out_arrived)
    own_out = reduce_out_z(join_x(out_kept, out_arrived))
    qkv_arrived = dp_swap(qkv_away, 1) if ringed() else None
    if ringed():
        d_norm1, qkv_arrived, cross_both, own_out, block_arrived, own_ffn = scatter_seq(
            partial, (qkv_arrived, cross_both, own_out, seq_swap(block_far, 2), own_ffn)
        )
        block_sum = block_near + block_arrived.astype(F32)
    else:
        d_norm1 = scatter_seq(partial)
    qkv_both = join_x(qkv_kept, qkv_arrived)
    own_qkv = reduce_dp_z(qkv_both)
    if ringed():
        qkv_both, cross_both = together(qkv_both, cross_both)
        cross_kept, cross_away = split_rows(cross_both)
        own_cross = join_x(cross_kept, x_swap(cross_away))
    else:
        block_sum, own_cross = scatter_seq(block_part), cross_both
    block = (after_cross + block_sum).astype(BF)
    normal_one, inv_one, _ = norm_forward(tokens.astype(F32), gain_one)
    back, gain_grad_one = norm_backward(d_norm1, normal_one, inv_one, gain_one)
    grad_in = d_after_self + back

    own_gate, own_up, own_down = part_hidden(own_ffn, 3)
    own_cross = collect(own_cross)
    own_out = head_rows_out(own_out)
    own_qkv = collect(own_qkv)
    g_q, g_k, g_v = (columns_back(own_qkv[:, :, i * mine : (i + 1) * mine]) for i in range(3))
    g_cq, g_ck, g_cv = (columns_back(own_cross[:, :, i * mine : (i + 1) * mine]) for i in range(3))
    gain_grads = all_sum(jnp.stack([gain_grad_one, gain_grad_two, gain_grad_three]))
    gain_grads = lax.dynamic_slice(gain_grads, (0, (d * n + s) * share), (3, share))

    def f32(x):
        return x.astype(F32)

    return (
        block.reshape(inputs.shape),
        grad_in.reshape(inputs.shape),
        grad_cond.reshape(conditioning.shape),
        gain_grads[0],
        gain_grads[1],
        gain_grads[2],
        f32(g_q),
        f32(g_k),
        f32(g_v),
        f32(own_out[:, :width]),
        f32(g_cq),
        f32(g_ck),
        f32(g_cv),
        f32(own_out[:, width:]),
        f32(own_gate),
        f32(own_up),
        f32(own_down),
    )


def solution(mesh):
    rows = P("dp", "seq", None)
    split = P(("dp", "seq"))
    matrix = P(("dp", "seq"), None)
    return jax.shard_map(
        per_device,
        mesh=mesh,
        in_specs=(rows, rows, P("dp"), P("dp"), split, split, split) + (matrix,) * 11 + (rows,),
        out_specs=(rows, rows, rows, split, split, split) + (matrix,) * 11,
        check_vma=False,
    )
```

```python
import functools
import math

import jax
import jax.numpy as jnp
from jax import lax
from jax.experimental import pallas as pl
from jax.experimental.layout import Layout, with_layout_constraint
from jax.experimental.pallas import tpu as pltpu
from jax.sharding import PartitionSpec as P

HEADS = 24
HEAD = 64
ROT = 32
EPSILON = 1e-05
BF = jnp.bfloat16
F32 = jnp.float32
PAIR = 2 * HEAD


def mm(left, right):
    return jnp.dot(left, right, preferred_element_type=F32)


def mm_t(left, right):
    return lax.dot_general(left, right, (((1,), (1,)), ((), ())), preferred_element_type=F32)


def t_mm(left, right):
    return lax.dot_general(left, right, (((0,), (0,)), ((), ())), preferred_element_type=F32)


def seq_swap(x, mask):
    n = lax.axis_size("seq")
    return lax.ppermute(x, "seq", [(i, i ^ mask) for i in range(n)])


def dp_swap(x, mask):
    n = lax.axis_size("dp")
    return lax.ppermute(x, "dp", [(i, i ^ mask) for i in range(n)])


def all_sum_dp(v):
    mask = lax.axis_size("dp") // 2
    while mask:
        v = v + dp_swap(v, mask)
        mask //= 2
    return v


def gather_seq(x, beside=()):
    core = seq_swap(x, 1)
    far = seq_swap(x, 2)
    if beside:
        far, *beside = together(far, *beside)
    diag = seq_swap(far, 1)
    blocks = jnp.stack([x, core, far, diag])
    return (blocks, *beside) if beside else blocks


def scatter_seq(partial, beside=()):
    far = partial[2].astype(F32) + seq_swap(partial[3], 1).astype(F32)
    arrived = seq_swap(far.astype(BF), 2)
    arrived, *beside = together(arrived, *beside)
    near = partial[0].astype(F32) + seq_swap(partial[1], 1).astype(F32)
    total = near + arrived.astype(F32)
    return (total, *beside) if beside else total


def x_swap(x):
    return dp_swap(x, 1)


def all_sum(v):
    for mask in (2, 1):
        v = v + seq_swap(v, mask)
    return all_sum_dp(v)


def natural(blocks):
    s = lax.axis_index("seq")
    n = lax.axis_size("seq")
    return [lax.dynamic_index_in_dim(blocks, k ^ s, 0, keepdims=False) for k in range(n)]


def gather_eight_first(x):
    return x, seq_swap(x, 2), x_swap(x)


def gather_eight(x):
    return gather_eight_last(*gather_eight_first(x))


def gather_eight_last(x, far, side):
    half = x.shape[0] // 2
    corner = jnp.concatenate([x_swap(far[:half]), seq_swap(side[half:], 2)])
    blocks = []
    for near in (x, far, side, corner):
        blocks += [near, seq_swap(near, 1)]
    return jnp.stack(blocks)


def scatter_eight(partial, first=None, second=None):
    half = partial.shape[1] // 2

    def with_core(k):
        return partial[k].astype(F32) + seq_swap(partial[k + 1], 1).astype(F32)

    corner = with_core(6).astype(BF)
    corner, partial = together(corner, partial)
    from_x, from_y = x_swap(corner[:half]), seq_swap(corner[half:], 2)
    out = []
    if first is not None:
        value = first(corner)
        from_x, from_y, value = together(from_x, from_y, value)
        out.append(value)
    far = with_core(2)
    far = jnp.concatenate([far[:half] + from_x.astype(F32), far[half:]]).astype(BF)
    side = with_core(4)
    side = jnp.concatenate([side[:half], side[half:] + from_y.astype(F32)]).astype(BF)
    far, side = together(far, side)
    from_y, from_x = seq_swap(far, 2), x_swap(side)
    if second is not None:
        value = second(far)
        from_y, from_x, value = together(from_y, from_x, value)
        out.append(value)
    return (with_core(0) + from_y.astype(F32) + from_x.astype(F32), *out)


def scatter_eight_x(partial):
    def with_core(k):
        return partial[k].astype(F32) + seq_swap(partial[k + 1], 1).astype(F32)

    away = jnp.stack([with_core(4).astype(BF), with_core(6).astype(BF)])
    arrived = x_swap(away)
    near = with_core(0) + arrived[0].astype(F32)
    return near, (with_core(2) + arrived[1].astype(F32)).astype(BF)


def together(*values):
    return lax.optimization_barrier(values)


RING_Z, RING_X = 4, 2


def ringed():
    return lax.axis_size("dp") == RING_Z * RING_X


def z_groups():
    return [[z * RING_X + x for z in range(RING_Z)] for x in range(RING_X)]


def gather_z(chunk):
    return lax.all_gather(chunk, "dp", axis=0, axis_index_groups=z_groups())


def gather_dp_z(chunk):
    if not ringed():
        return lax.all_gather(chunk, "dp", axis=0, tiled=True)
    return gather_z(chunk)


def pair_x(chunk):
    if not ringed():
        return chunk
    other = x_swap(chunk)
    first = lax.axis_index("dp") % RING_X == 0
    return jnp.concatenate([jnp.where(first, chunk, other), jnp.where(first, other, chunk)])


def gather_dp_x(own, other=None):
    if not ringed():
        return own
    cols = own.shape[2]
    first = lax.axis_index("dp") % RING_X == 0
    other = dp_swap(own, 1) if other is None else other
    both = jnp.stack([jnp.where(first, own, other), jnp.where(first, other, own)], axis=1)
    return both.reshape(-1, cols)


def reduce_dp_x(slots):
    kept, away = split_x(slots)
    return join_x(kept, x_swap(away) if ringed() else None)


def split_x(slots):
    n, rows, cols = slots.shape
    if not ringed():
        return slots, slots
    xx = lax.axis_index("dp") % RING_X
    split = slots.reshape(RING_Z, RING_X, rows, cols)
    away = lax.dynamic_index_in_dim(split, 1 - xx, axis=1, keepdims=False)
    kept = lax.dynamic_index_in_dim(split, xx, axis=1, keepdims=False)
    return kept, away


def join_x(kept, arrived):
    if ringed():
        kept = (kept.astype(F32) + arrived.astype(F32)).astype(BF)
    return kept.reshape(-1, kept.shape[-1])


def reduce_dp_z(both):
    if not ringed():
        return lax.psum_scatter(both, "dp", scatter_dimension=0, tiled=True)
    return lax.psum_scatter(
        both, "dp", scatter_dimension=0, tiled=True, axis_index_groups=z_groups()
    )


def reduce_dp(slots):
    return reduce_dp_z(reduce_dp_x(slots))


def wide():
    return lax.axis_size("seq") * (RING_X if ringed() else 1)


def hidden_out(mats):
    n = lax.axis_size("seq")
    parts = wide() // n
    rows = mats[0].shape[0]
    cut = [m.reshape(rows, n, parts, -1) for m in mats]
    return jnp.concatenate(cut, axis=3).transpose(1, 0, 2, 3).reshape(n, rows, -1)


def deal_hidden_x(got):
    if not ringed():
        return got
    rows = got.shape[0]
    xx = lax.axis_index("dp") % RING_X
    cut = got.reshape(rows, RING_X, -1)
    kept = lax.dynamic_index_in_dim(cut, xx, 1, keepdims=False)
    arrived = x_swap(lax.dynamic_index_in_dim(cut, 1 - xx, 1, keepdims=False))
    first = xx == 0
    return jnp.concatenate([jnp.where(first, kept, arrived), jnp.where(first, arrived, kept)])


def gather_hidden(x):
    if not ringed():
        return lax.all_gather(x, "dp", axis=0, tiled=True)
    return lax.all_gather(x, "dp", axis=0, tiled=True, axis_index_groups=z_groups())


def reduce_hidden(grad):
    if not ringed():
        return lax.psum_scatter(grad, "dp", scatter_dimension=0, tiled=True)
    return lax.psum_scatter(
        grad, "dp", scatter_dimension=0, tiled=True, axis_index_groups=z_groups()
    )


def split_rows(x):
    xx = lax.axis_index("dp") % RING_X
    cut = x.reshape(RING_X, -1, x.shape[1])
    kept = lax.dynamic_index_in_dim(cut, xx, 0, keepdims=False)
    return kept, lax.dynamic_index_in_dim(cut, 1 - xx, 0, keepdims=False)


def join_hidden(kept, arrived):
    first = lax.axis_index("dp") % RING_X == 0
    return jnp.concatenate(
        [jnp.where(first, kept, arrived), jnp.where(first, arrived, kept)], axis=1
    )


def part_hidden(got, count):
    n = lax.axis_size("seq")
    parts = wide() // n
    rows = got.shape[1]
    got = got.reshape(n, rows, parts, count, -1)
    return [got[:, :, :, i].transpose(1, 0, 2, 3).reshape(rows, -1) for i in range(count)]


def columns_out(x):
    rows = x.shape[0]
    n = lax.axis_size("seq")
    return x.reshape(rows, HEADS // n, n, HEAD).transpose(2, 0, 1, 3).reshape(n, rows, -1)


def columns_back(x):
    n, rows, _ = x.shape
    return x.reshape(n, rows, HEADS // n, HEAD).transpose(1, 2, 0, 3).reshape(rows, HEADS * HEAD)


def deal(x):
    got = lax.all_to_all(x, "seq", split_axis=0, concat_axis=0, tiled=True)
    return got.reshape(-1, x.shape[-1])


def collect(x):
    n = lax.axis_size("seq")
    return lax.all_to_all(
        x.reshape(n, -1, x.shape[-1]), "seq", split_axis=0, concat_axis=0, tiled=True
    )


def head_slot():
    s, d = lax.axis_index("seq"), lax.axis_index("dp")
    n = lax.axis_size("seq")
    per = HEADS // lax.axis_size("dp")
    return (s + (n - per % n) * d) % n, per, n


def slot_place(d):
    s = lax.axis_index("seq")
    n = lax.axis_size("seq")
    per = HEADS // lax.axis_size("dp")
    j = (s + (n - per % n) * d) % n
    return jnp.where(j < per, (per * d + j - s) // n, HEADS // n)


def head_piece(x):
    if not ringed():
        return x
    rows = natural(gather_seq(x))
    rows = jnp.concatenate(rows + [jnp.zeros((HEAD, x.shape[1]), x.dtype)])
    return lax.dynamic_slice(rows, (head_slot()[0] * HEAD, 0), (HEAD, x.shape[1]))


def gather_head_rows(piece):
    n = lax.axis_size("seq")
    s = lax.axis_index("seq")
    rows, cols = piece.shape
    mine = HEADS // n
    if not ringed():
        full = lax.all_gather(piece, ("dp", "seq"), axis=0, tiled=True)
        picked = lax.dynamic_index_in_dim(full.reshape(mine, n, HEAD, cols), s, 1, keepdims=False)
        return picked.reshape(mine * HEAD, cols)
    owners = gather_z(pair_x(piece)).reshape(RING_Z * RING_X, HEAD, cols)
    per = head_slot()[1]
    return jnp.concatenate(
        [
            lax.dynamic_index_in_dim(owners, (n * p + s) // per, 0, keepdims=False)
            for p in range(mine)
        ]
    )


def split_head_rows(x):
    n = lax.axis_size("seq")
    s = lax.axis_index("seq")
    cols = x.shape[1]
    mine = HEADS // n
    if not ringed():
        full = jnp.zeros((mine, n, HEAD, cols), BF)
        full = lax.dynamic_update_index_in_dim(full, x.reshape(mine, 1, HEAD, cols), s, 1)
        return full.reshape(-1, cols), full.reshape(-1, cols)
    padded = jnp.concatenate([x, jnp.zeros((HEAD, cols), x.dtype)])
    slots = jnp.stack(
        [
            lax.dynamic_slice(padded, (slot_place(d) * HEAD, 0), (HEAD, cols))
            for d in range(lax.axis_size("dp"))
        ]
    )
    return split_x(slots)


def reduce_out_z(both):
    if not ringed():
        return lax.psum_scatter(both, ("dp", "seq"), scatter_dimension=0, tiled=True)
    return reduce_dp_z(both)


def head_rows_out(own):
    n = lax.axis_size("seq")
    s = lax.axis_index("seq")
    size = lax.axis_size("dp")
    cols = own.shape[-1]
    if not ringed():
        return own.astype(F32)
    pieces = gather_seq(own)
    per = HEADS // size
    d = lax.axis_index("dp")
    rows = jnp.concatenate(
        [
            lax.dynamic_index_in_dim(pieces, ((per * d + j) % n) ^ s, 0, keepdims=False)
            for j in range(per)
        ]
    )
    share = per * HEAD // n
    return lax.dynamic_slice(rows, (s * share, 0), (share, cols)).astype(F32)


def norm_forward(values, gain_vec):
    average = jnp.mean(values, axis=-1, keepdims=True)
    centred = values - average
    variance = jnp.mean(centred * centred, axis=-1, keepdims=True)
    inv_std = lax.rsqrt(variance + EPSILON)
    normal = centred * inv_std
    return normal, inv_std, (normal * gain_vec).astype(BF)


def norm_backward(grad_normed, normal, inv_std, gain_vec):
    grad_gain = jnp.sum(grad_normed * normal, axis=0)
    grad_hat = grad_normed * gain_vec
    mean_hat = jnp.mean(grad_hat, axis=-1, keepdims=True)
    mean_mix = jnp.mean(grad_hat * normal, axis=-1, keepdims=True)
    return inv_std * (grad_hat - mean_hat - normal * mean_mix), grad_gain


def flat(ref):
    value = ref[...]
    return value.reshape(value.shape[0] * value.shape[1] * value.shape[2], value.shape[3])


def turn(m, cos, up, down):
    return m * cos + pltpu.roll(m, PAIR - ROT // 2, 1) * up + pltpu.roll(m, ROT // 2, 1) * down


SCALE = 1.0 / math.sqrt(HEAD)


def soft(q, k, ok):
    scores = mm_t(q, k) * SCALE
    scores = jnp.where(ok > 0.0, scores, -1e30)
    top = jnp.max(scores, axis=-1, keepdims=True)
    e = jnp.exp(scores - top)
    return e * (1.0 / jnp.sum(e, axis=-1, keepdims=True))


def self_forward_kernel(ok_ref, cos_ref, up_ref, down_ref, q_ref, k_ref, v_ref, o_ref, qr_ref, kr_ref, vr_ref):
    cos, up, down = (r[...].reshape(-1, PAIR) for r in (cos_ref, up_ref, down_ref))
    q = turn(flat(q_ref), cos, up, down).astype(BF)
    k = turn(flat(k_ref), cos, up, down).astype(BF)
    v = flat(v_ref).astype(BF)
    ok = ok_ref[0]
    outs = []
    for h in (0, 1):
        sl = slice(h * HEAD, (h + 1) * HEAD)
        p = soft(q[:, sl], k[:, sl], ok).astype(BF)
        outs.append(mm(p, v[:, sl]))
    o_ref[...] = jnp.concatenate(outs, axis=1).astype(BF).reshape(o_ref.shape)
    qr_ref[...] = q.reshape(qr_ref.shape)
    kr_ref[...] = k.reshape(kr_ref.shape)
    vr_ref[...] = v.reshape(vr_ref.shape)


def pair_back(q, k, v, g, ok):
    dqs, dks, dvs = [], [], []
    for h in (0, 1):
        sl = slice(h * HEAD, (h + 1) * HEAD)
        p = soft(q[:, sl], k[:, sl], ok)
        dp = mm_t(g[:, sl], v[:, sl])
        inner = jnp.sum(p * dp, axis=-1, keepdims=True)
        ds = (p * (dp - inner)).astype(BF)
        dqs.append(mm(ds, k[:, sl]) * SCALE)
        dks.append(t_mm(ds, q[:, sl]) * SCALE)
        dvs.append(t_mm(p.astype(BF), g[:, sl]))
    return [jnp.concatenate(t, axis=1) for t in (dqs, dks, dvs)]


def self_backward_kernel(ok_ref, cos_ref, up_ref, down_ref, q_ref, k_ref, v_ref, g_ref, o_ref):
    cos, up, down = (r[...].reshape(-1, PAIR) for r in (cos_ref, up_ref, down_ref))
    dq, dk, dv = pair_back(flat(q_ref), flat(k_ref), flat(v_ref), flat(g_ref), ok_ref[0])
    dq = turn(dq, cos, -up, -down)
    dk = turn(dk, cos, -up, -down)
    pairs = o_ref.shape[3] // (3 * PAIR)
    hp = pl.program_id(1)
    shape = o_ref.shape[:3] + (PAIR,)
    for which, value in enumerate((dq, dk, dv)):
        at = pl.ds(pl.multiple_of((which * pairs + hp) * PAIR, PAIR), PAIR)
        o_ref[:, :, :, at] = value.astype(BF).reshape(shape)


def cross_forward_kernel(ok_ref, q_ref, k_ref, v_ref, o_ref):
    q, k, v = flat(q_ref), flat(k_ref), flat(v_ref)
    ok = ok_ref[0]
    outs = []
    for h in (0, 1):
        sl = slice(h * HEAD, (h + 1) * HEAD)
        p = soft(q[:, sl], k[:, sl], ok).astype(BF)
        outs.append(mm(p, v[:, sl]))
    o_ref[...] = jnp.concatenate(outs, axis=1).astype(BF).reshape(o_ref.shape)


def cross_backward_kernel(ok_ref, q_ref, k_ref, v_ref, g_ref, dq_ref, dkv_ref):
    dq, dk, dv = pair_back(flat(q_ref), flat(k_ref), flat(v_ref), flat(g_ref), ok_ref[0])
    dq_ref[...] = dq.astype(BF).reshape(dq_ref.shape)
    pairs = dkv_ref.shape[3] // (2 * PAIR)
    hp = pl.program_id(1)
    shape = dkv_ref.shape[:3] + (PAIR,)
    for which, value in enumerate((dk, dv)):
        at = pl.ds(pl.multiple_of((which * pairs + hp) * PAIR, PAIR), PAIR)
        dkv_ref[:, :, :, at] = value.astype(BF).reshape(shape)


def pair_spec(x, offset=0):
    r, _, t, _ = x.shape
    return pl.BlockSpec((r, 1, t, PAIR), lambda b, hp: (0, b, 0, offset + hp))


def wide_spec(r, t, width):
    return pl.BlockSpec((r, 1, t, width), lambda b, hp: (0, b, 0, 0))


def ok_spec(ok):
    return pl.BlockSpec((1, 1, ok.shape[2]), lambda b, hp: (b, 0, 0))


def table_spec(table):
    return pl.BlockSpec(table.shape, lambda b, hp: (0, 0, 0))


def cost(x, keys, products):
    r, b, t, width = x.shape
    return pl.CostEstimate(
        flops=2 * r * b * t * width * keys * products * 2,
        bytes_accessed=8 * x.size,
        transcendentals=r * b * t * keys * (width // HEAD),
    )


def self_forward(ok, tables, qk, v):
    r, b, t, width = v.shape
    pairs = width // PAIR
    shape = jax.ShapeDtypeStruct((r, b, t, pairs * PAIR), BF)
    return pl.pallas_call(
        self_forward_kernel,
        grid=(b, pairs),
        in_specs=[ok_spec(ok)]
        + [table_spec(x) for x in tables]
        + [pair_spec(qk), pair_spec(qk, pairs), pair_spec(v)],
        out_specs=[pair_spec(shape)] * 4,
        out_shape=[shape] * 4,
        cost_estimate=cost(shape, r * t, 2),
        name="self_forward",
    )(ok, *tables, qk, qk, v)


def self_backward(ok, tables, q, k, v, g):
    r, b, t, width = q.shape
    pairs = width // PAIR
    return pl.pallas_call(
        self_backward_kernel,
        grid=(b, pairs),
        in_specs=[ok_spec(ok)] + [table_spec(x) for x in tables] + [pair_spec(q)] * 4,
        out_specs=wide_spec(r, t, 3 * width),
        out_shape=jax.ShapeDtypeStruct((r, b, t, 3 * width), BF),
        cost_estimate=cost(q, r * t, 5),
        name="self_backward",
    )(ok, *tables, q, k, v, g)


def cross_forward(ok, q, kv):
    r, b, t, width = q.shape
    pairs = width // PAIR
    return pl.pallas_call(
        cross_forward_kernel,
        grid=(b, pairs),
        in_specs=[ok_spec(ok), pair_spec(q), pair_spec(kv), pair_spec(kv, pairs)],
        out_specs=pair_spec(q),
        out_shape=jax.ShapeDtypeStruct(q.shape, BF),
        cost_estimate=cost(q, r * kv.shape[2], 2),
        name="cross_forward",
    )(ok, q, kv, kv)


def cross_backward(ok, q, kv, g):
    r, b, t, width = q.shape
    pairs = width // PAIR
    return pl.pallas_call(
        cross_backward_kernel,
        grid=(b, pairs),
        in_specs=[ok_spec(ok), pair_spec(q), pair_spec(kv), pair_spec(kv, pairs), pair_spec(q)],
        out_specs=[pair_spec(q), wide_spec(r, kv.shape[2], kv.shape[3])],
        out_shape=[jax.ShapeDtypeStruct(q.shape, BF), jax.ShapeDtypeStruct(kv.shape, BF)],
        cost_estimate=cost(q, r * kv.shape[2], 5),
        name="cross_backward",
    )(ok, q, kv, kv, g)


def per_device(
    inputs,
    conditioning,
    seq_lengths,
    cond_lengths,
    gain_self,
    gain_cross,
    gain_mlp,
    w_query,
    w_key,
    w_value,
    w_output,
    c_query,
    c_key,
    c_value,
    c_output,
    w_gate,
    w_up,
    w_down,
    cotangent,
):
    batch, tokens_dev, width = inputs.shape
    cond_dev = conditioning.shape[1]
    n = lax.axis_size("seq")
    dp = lax.axis_size("dp")
    s = lax.axis_index("seq")
    d = lax.axis_index("dp")
    rel = jnp.arange(n) ^ s
    mine = width // n

    positions = rel[:, None] * tokens_dev + jnp.arange(tokens_dev)[None, :]
    key_ok = (positions.reshape(1, 1, -1) < seq_lengths[:, None, None]).astype(F32)
    cond_pos = rel[:, None] * cond_dev + jnp.arange(cond_dev)[None, :]
    cond_ok = (cond_pos.reshape(1, 1, -1) < cond_lengths[:, None, None]).astype(F32)
    half = ROT // 2
    inverse = 10000.0 ** (-jnp.arange(half).astype(F32) / half)
    angles = positions.astype(F32)[:, :, None] * inverse
    cosine, sine = jnp.cos(angles), jnp.sin(angles)
    one, nil = jnp.ones(cosine.shape[:2] + (HEAD - ROT,), F32), jnp.zeros_like(cosine)
    nil_rest = jnp.zeros_like(one)
    tables = [
        jnp.concatenate(parts + parts, axis=-1)
        for parts in (
            [cosine, cosine, one],
            [-sine, nil, nil_rest],
            [nil, sine, nil_rest],
        )
    ]

    gain_rows = jnp.stack([gain_self, gain_cross, gain_mlp]).astype(F32)
    share = gain_rows.shape[1]
    placed = lax.dynamic_update_slice(jnp.zeros((3, width), F32), gain_rows, (0, (d * n + s) * share))
    placed = placed + seq_swap(placed, 2)
    rows = batch * tokens_dev
    total = n * rows

    def cut(*mats):
        return jnp.concatenate([columns_out(w) for w in mats], axis=2)

    qk_part = deal(cut(w_query, w_key))
    qk_part, w_value, c_query, w_output, c_output = together(
        qk_part, w_value, c_query, w_output, c_output
    )

    qk_z = gather_dp_z(qk_part)
    vcq_z = gather_dp_z(deal(cut(w_value, c_query)))
    piece = head_piece(jnp.concatenate([w_output, c_output], axis=1))
    out_w = gather_head_rows(piece)
    qk_z, placed, tokens, given, c_key, c_value, w_gate, w_up, w_down = together(
        qk_z,
        placed,
        inputs.reshape(rows, width),
        conditioning.reshape(batch * cond_dev, width),
        c_key,
        c_value,
        w_gate,
        w_up,
        w_down,
    )
    qk_w = gather_dp_x(qk_z)
    gains = all_sum_dp(placed + seq_swap(placed, 1))
    tokens_all = gather_seq(tokens)
    gain_one, gain_two, gain_three = gains[0], gains[1], gains[2]
    ckv_z = gather_dp_z(deal(cut(c_key, c_value)))
    ffn_part = deal(hidden_out([w_gate, w_up, w_down]))
    cond_all = gather_seq(given).reshape(-1, width)
    hid = w_gate.shape[1] // wide()
    gather_ffn = gather_eight if ringed() else gather_seq
    shared = wide()

    normed_one = norm_forward(tokens_all.reshape(total, width).astype(F32), gain_one)[2]
    vcq_w = gather_dp_x(vcq_z)
    v_w, cq_w = vcq_w[:, :mine], vcq_w[:, mine:]
    qk = mm(normed_one, qk_w).reshape(n, batch, tokens_dev, 2 * mine)
    v_own = mm(normed_one, v_w).reshape(n, batch, tokens_dev, mine)
    qk, v_own, ffn_part = together(qk, v_own, ffn_part)
    attended, q_rot, k_rot, v_low = self_forward(key_ok, tables, qk, v_own)
    attended = attended.reshape(total, mine)
    ffn_w = deal_hidden_x(ffn_part)
    gu_w = gather_hidden(ffn_w[:, : 2 * hid])
    down_w = gather_hidden(ffn_w[:, 2 * hid :])
    attended, ffn_w, out_w = together(attended, ffn_w, out_w)
    w_out, c_out = out_w[:, :width], out_w[:, width:]
    partial = mm(attended, w_out).astype(BF).reshape(n, rows, width)
    partial, ckv_z = scatter_seq(partial, (ckv_z,))
    after_self = tokens.astype(F32) + partial
    normal_two, inv_two, own_two = norm_forward(after_self, gain_two)
    if ringed():
        normed_two, ckv_other = gather_seq(own_two, (x_swap(ckv_z),))
        ckv_w = gather_dp_x(ckv_z, ckv_other)
    else:
        normed_two, ckv_w = gather_seq(own_two), ckv_z
    normed_two = normed_two.reshape(total, width)
    cq = mm(normed_two, cq_w).astype(BF).reshape(n, batch, tokens_dev, mine)
    ckv = mm(cond_all, ckv_w).astype(BF).reshape(n, batch, cond_dev, 2 * mine)
    cq, incoming = together(cq, cotangent.reshape(rows, width))
    cross_att = cross_forward(cond_ok, cq, ckv).reshape(total, mine)
    if ringed():
        cross_att, *incoming_first = together(cross_att, *gather_eight_first(incoming))
    partial = mm(cross_att, c_out).astype(BF).reshape(n, rows, width)
    after_cross = after_self + scatter_seq(partial)
    after_cross, gu_w = together(after_cross, gu_w)
    normal_three, inv_three, own_three = norm_forward(after_cross, gain_three)
    normed_three = gather_ffn(own_three).reshape(shared * rows, width)
    if ringed():
        normed_three, *incoming_first = together(normed_three, *incoming_first)
        incoming_all = gather_eight_last(*incoming_first).reshape(shared * rows, width)
    else:
        incoming_all = gather_seq(incoming).reshape(total, width)
    gate = mm(normed_three, gu_w[:, :hid])
    gate, incoming_all = together(gate, incoming_all)
    up = mm(normed_three, gu_w[:, hid:])
    sig = jax.nn.sigmoid(gate)
    hidden = (gate * sig * up).astype(BF)
    grad_down = t_mm(incoming_all, hidden).astype(BF)
    incoming_all, grad_down = together(incoming_all, grad_down)
    d_hidden = mm(incoming_all, down_w)
    d_gate = (d_hidden * up * sig * (1.0 + gate * (1.0 - sig))).astype(BF)
    d_up = (d_hidden * gate * sig).astype(BF)
    d_gu = jnp.concatenate([d_gate, d_up], axis=1)
    own_down = reduce_hidden(grad_down)
    partial = mm_t(d_gu, gu_w).astype(BF).reshape(shared, rows, width)

    def block_product(now):
        _, late = together(now, hidden)
        return mm_t(late, down_w).astype(BF).reshape(shared, rows, width)

    def gu_product(now):
        _, late = together(now, d_gu)
        return t_mm(normed_three, late).astype(BF)

    if ringed():
        d_norm3, block_part, grad_gu = scatter_eight(partial, block_product, gu_product)
    else:
        d_norm3 = scatter_seq(partial)
        block_part, grad_gu = block_product(partial), gu_product(partial)
    d_norm3, own_down = together(d_norm3, own_down)
    own_gu = reduce_hidden(grad_gu)
    back, gain_grad_three = norm_backward(d_norm3, normal_three, inv_three, gain_three)
    d_after_cross = incoming.astype(F32) + back
    dc_low = gather_seq(d_after_cross.astype(BF)).reshape(total, width)
    d_catt = mm_t(dc_low, c_out).astype(BF).reshape(n, batch, tokens_dev, mine)
    grad_c_out = t_mm(cross_att, dc_low).astype(BF)
    d_cq, d_ckv = cross_backward(cond_ok, cq, ckv, d_catt)
    d_cq = d_cq.reshape(total, mine)
    d_ckv = d_ckv.reshape(n * batch * cond_dev, 2 * mine)
    partial = mm_t(d_cq, cq_w).astype(BF).reshape(n, rows, width)
    grad_cross = jnp.concatenate([t_mm(normed_two, d_cq), t_mm(cond_all, d_ckv)], axis=1).astype(BF)
    grad_cross = with_layout_constraint(grad_cross, Layout(major_to_minor=(0, 1)))
    d_norm2, grad_cross = scatter_seq(partial, (grad_cross,))
    cross_both = reduce_hidden(grad_cross)
    partial = mm_t(d_ckv, ckv_w).astype(BF).reshape(n, batch * cond_dev, width)
    grad_cond = scatter_seq(partial)
    back, gain_grad_two = norm_backward(d_norm2, normal_two, inv_two, gain_two)
    d_after_self = d_after_cross + back
    if ringed():
        block_near, block_far = scatter_eight_x(block_part)
        ds_low, block_near, block_far = gather_seq(
            d_after_self.astype(BF), (block_near, block_far)
        )
    else:
        ds_low = gather_seq(d_after_self.astype(BF))
    ds_low = ds_low.reshape(total, width)
    ds_low, own_gu, own_down = together(ds_low, own_gu, own_down)
    own_ffn = jnp.concatenate([own_gu, own_down], axis=1)
    if ringed():
        ffn_kept, ffn_away = split_rows(own_ffn)
        ffn_arrived = x_swap(ffn_away)
    ds_low, grad_c_out = together(ds_low, grad_c_out)
    d_att = mm_t(ds_low, w_out).astype(BF).reshape(n, batch, tokens_dev, mine)
    grad_out = t_mm(attended, ds_low).astype(BF)
    out_kept, out_away = split_head_rows(jnp.concatenate([grad_out, grad_c_out], axis=1))
    d_att, out_kept, out_away = together(d_att, out_kept, out_away)
    out_arrived = x_swap(out_away) if ringed() else out_away
    d_qkv = self_backward(key_ok, tables, q_rot, k_rot, v_low, d_att).reshape(total, 3 * mine)
    if ringed():
        d_qkv, ffn_arrived = together(d_qkv, ffn_arrived)
        own_ffn = join_hidden(ffn_kept, ffn_arrived)
    own_ffn = collect(own_ffn)
    grad_qkv = t_mm(normed_one, d_qkv).astype(BF)
    d_qkv, grad_qkv = together(d_qkv, grad_qkv)
    qkv_kept, qkv_away = split_x(grad_qkv.reshape(dp, width // dp, grad_qkv.shape[1]))
    qkv_away, d_qkv = together(qkv_away, d_qkv)
    partial = mm_t(d_qkv, jnp.concatenate([qk_w, v_w], axis=1))
    partial = partial.astype(BF).reshape(n, rows, width)
    partial, out_arrived = together(partial, out_arrived)
    own_out = reduce_out_z(join_x(out_kept, out_arrived))
    qkv_arrived = dp_swap(qkv_away, 1) if ringed() else None
    if ringed():
        d_norm1, qkv_arrived, cross_both, own_out, block_arrived, own_ffn = scatter_seq(
            partial, (qkv_arrived, cross_both, own_out, seq_swap(block_far, 2), own_ffn)
        )
        block_sum = block_near + block_arrived.astype(F32)
    else:
        d_norm1 = scatter_seq(partial)
    qkv_both = join_x(qkv_kept, qkv_arrived)
    own_qkv = reduce_dp_z(qkv_both)
    if ringed():
        qkv_both, cross_both = together(qkv_both, cross_both)
        cross_kept, cross_away = split_rows(cross_both)
        own_cross = join_x(cross_kept, x_swap(cross_away))
    else:
        block_sum, own_cross = scatter_seq(block_part), cross_both
    block = (after_cross + block_sum).astype(BF)
    normal_one, inv_one, _ = norm_forward(tokens.astype(F32), gain_one)
    back, gain_grad_one = norm_backward(d_norm1, normal_one, inv_one, gain_one)
    grad_in = d_after_self + back

    own_gate, own_up, own_down = part_hidden(own_ffn, 3)
    own_cross = collect(own_cross)
    own_out = head_rows_out(own_out)
    own_qkv = collect(own_qkv)
    g_q, g_k, g_v = (columns_back(own_qkv[:, :, i * mine : (i + 1) * mine]) for i in range(3))
    g_cq, g_ck, g_cv = (columns_back(own_cross[:, :, i * mine : (i + 1) * mine]) for i in range(3))
    gain_grads = all_sum(jnp.stack([gain_grad_one, gain_grad_two, gain_grad_three]))
    gain_grads = lax.dynamic_slice(gain_grads, (0, (d * n + s) * share), (3, share))

    def f32(x):
        return x.astype(F32)

    return (
        block.reshape(inputs.shape),
        grad_in.reshape(inputs.shape),
        grad_cond.reshape(conditioning.shape),
        gain_grads[0],
        gain_grads[1],
        gain_grads[2],
        f32(g_q),
        f32(g_k),
        f32(g_v),
        f32(own_out[:, :width]),
        f32(g_cq),
        f32(g_ck),
        f32(g_cv),
        f32(own_out[:, width:]),
        f32(own_gate),
        f32(own_up),
        f32(own_down),
    )


def solution(mesh):
    rows = P("dp", "seq", None)
    split = P(("dp", "seq"))
    matrix = P(("dp", "seq"), None)
    return jax.shard_map(
        per_device,
        mesh=mesh,
        in_specs=(rows, rows, P("dp"), P("dp"), split, split, split) + (matrix,) * 11 + (rows,),
        out_specs=(rows, rows, rows, split, split, split) + (matrix,) * 11,
        check_vma=False,
    )
```
